32 devices in a mesh: vol: 8 (over z, x), rep: 4 (over y, core).
Axes of the slice: x: 2, y: 2, z: 4, core: 2. Of those that a mesh axis runs over, the one named last changes fastest.
Arguments:
- cutouts: bfloat16 [4, 256, 4096], P('rep', 'vol'), may hold values from -6 to 6
- counts: int32 [4, 8], P('rep', 'vol'), may hold values from 1 to 32, as said below
- partner: int32 [4, 128], P('rep'), may hold values from 0 to 127, as said below
- w_stem: bfloat16 [64, 128], replicated, may hold values from -0.75 to 0.75
- w_mix: bfloat16 [128, 128], replicated, may hold values from -0.5 to 0.5
- w_out: bfloat16 [128, 128], replicated, may hold values from -0.5 to 0.5
- w_proj: bfloat16 [128, 64], replicated, may hold values from -0.5 to 0.5
Outputs:
- upd_stem: float32 [64, 128], replicated
- upd_mix: float32 [128, 128], replicated
- upd_out: float32 [128, 128], replicated
- upd_proj: float32 [128, 64], replicated
- node_loss: float32 [4, 8, 16], P('rep', 'vol')
The draws below stay inside these ranges and needn't reach their ends.
Inputs may be any that keep to these rules, and one draw needn't show every extreme that they name: `counts`: each row sums to 128, and its largest entry is exactly 32. Each row pairs the nodes of a group: partner[r, partner[r, g]] = g and partner[r, g] != g.
All inputs are finite; a program needn't handle non-finite values.
Results may differ from the reference program's by a relative error of at most 0.0035.
Values may be sent and summed in bfloat16 or wider, within the bound.
No kernel may reach another device: no remote copies, remote signals or barrier semaphores. Data moves between devices by JAX's collectives and lax.ppermute only.
A program may use at most 64 MiB of HBM per device.

```python
import jax
import jax.numpy as jnp
from jax import lax

C = 128
E = 64
VOXP = 64
PATCH = 64
NODE_DEV = 16
MAXN = 32
NODES = 128
N_VOL = 8
N_REP = 4


pattern_kinds = 12


def owner_counts(key):
    keys = jax.random.split(key, N_REP)

    def one_group(group_key):
        order_key, moves_key = jax.random.split(group_key)
        order = jax.random.permutation(order_key, N_VOL).astype(jnp.int32)
        moves = jax.random.randint(moves_key, (N_VOL,), 0, NODE_DEV, dtype=jnp.int32)
        position = jnp.arange(N_VOL, dtype=jnp.int32)
        beyond = position - 3
        pair_slot = jnp.clip(beyond // 2, 0, N_VOL - 1)
        amount = jnp.take(moves, pair_slot)
        mate = jnp.where(beyond % 2 == 0, position + 1, position - 1)
        paired = (beyond >= 0) & (mate < N_VOL)
        signed = jnp.where(beyond % 2 == 0, amount, -amount)
        values = NODE_DEV + jnp.where(paired, signed, 0)
        values = jnp.where(position == 0, MAXN, values)
        values = jnp.where(position == 1, 1, values)
        values = jnp.where(position == 2, NODE_DEV - 1, values)
        return jnp.zeros((N_VOL,), jnp.int32).at[order].set(values.astype(jnp.int32))
    return jax.vmap(one_group)(keys)


def draw_counts(key, part):
    return owner_counts(jax.random.fold_in(key, 29))


def draw_cutouts(key, part):
    group_counts = owner_counts(jax.random.fold_in(key, 29))
    offsets = (jnp.cumsum(group_counts, axis=1) - group_counts).astype(jnp.int32)
    slot = jnp.arange(MAXN, dtype=jnp.int32)
    node = (offsets[:, :, None] + slot[None, None, :]).reshape(N_REP, N_VOL * MAXN)
    kind = node % N_VOL % pattern_kinds
    pattern_key, single_key, noise_key = jax.random.split(jax.random.fold_in(key, 31), 3)
    patterns = 2.0 * jax.random.normal(pattern_key, (pattern_kinds, VOXP), jnp.float32)
    shared = jnp.take(patterns, kind, axis=0)
    single = jax.random.normal(single_key, (N_REP, N_VOL * MAXN, VOXP), jnp.float32)
    noise = jax.random.normal(noise_key, (N_REP, N_VOL * MAXN, PATCH, VOXP), jnp.float32)
    values = jnp.clip(shared[:, :, None, :] + single[:, :, None, :] + noise, -6.0, 6.0)
    return values.reshape(N_REP, N_VOL * MAXN, PATCH * VOXP).astype(jnp.bfloat16)


def draw_partner(key, part):
    keys = jax.random.split(jax.random.fold_in(key, 17), N_REP)

    def one_group(group_key):
        order = jax.random.permutation(group_key, NODES).astype(jnp.int32)
        pairs = order.reshape(NODES // 2, 2)
        paired = jnp.zeros((NODES,), jnp.int32)
        paired = paired.at[pairs[:, 0]].set(pairs[:, 1])
        paired = paired.at[pairs[:, 1]].set(pairs[:, 0])
        return paired
    return jax.vmap(one_group)(keys)


def centred(own_key, dims, spread, limit, kind=jnp.bfloat16):
    drawn = jax.random.normal(own_key, dims, jnp.float32) * spread
    return jnp.minimum(jnp.maximum(drawn, -limit), limit).astype(kind)


def setup_inputs(seed: int = 0) -> dict:
    arg_keys = jax.random.split(jax.random.key(seed), 8)
    cutouts = draw_cutouts(jax.random.fold_in(arg_keys[7], 71), 0)
    counts = draw_counts(jax.random.fold_in(arg_keys[7], 71), 0)
    partner = draw_partner(jax.random.fold_in(arg_keys[7], 71), 0)
    w_stem = centred(arg_keys[3], (VOXP, C), VOXP ** -0.5, 0.75)
    w_mix = centred(arg_keys[4], (C, C), C ** -0.5, 0.5)
    w_out = centred(arg_keys[5], (C, C), C ** -0.5, 0.5)
    w_proj = centred(arg_keys[6], (C, E), C ** -0.5, 0.5)
    return {"cutouts": cutouts, "counts": counts, "partner": partner, "w_stem": w_stem, "w_mix": w_mix, "w_out": w_out, "w_proj": w_proj}


logit_divisor_factor = 0.2
norm_eps = 1e-06
rms_eps = 1e-06

def first_dot(left, right):
    return lax.dot_general(left, right, (((0,), (0,)), ((), ())), preferred_element_type=jnp.float32)

def concluding_matrix_multiply(left, right):
    return lax.dot_general(left, right, (((1,), (1,)), ((), ())), preferred_element_type=jnp.float32)

def silu_slope(value):
    sigma = jax.nn.sigmoid(value)
    return sigma * (1.0 + value * (1.0 - sigma))

def encode(cutout_rows, w_stem, w_mix, w_out, w_proj):
    number = cutout_rows.shape[0]
    patches = cutout_rows.reshape(-1, w_stem.shape[0])
    per_cutout = patches.shape[0] // number
    pre_stem = jnp.dot(patches, w_stem, preferred_element_type=jnp.float32)
    hidden = jax.nn.silu(pre_stem).astype(jnp.bfloat16)
    pre_mix = jnp.dot(hidden, w_mix, preferred_element_type=jnp.float32)
    mixed = jax.nn.silu(pre_mix).astype(jnp.bfloat16)
    summed = hidden.astype(jnp.float32) + jnp.dot(mixed, w_out, preferred_element_type=jnp.float32)
    pooled = lax.optimization_barrier(jnp.mean(summed.reshape(number, per_cutout, -1), axis=1)).astype(jnp.bfloat16)
    raw_embed = jnp.dot(pooled, w_proj, preferred_element_type=jnp.float32)
    inv_norm = lax.rsqrt(lax.optimization_barrier(jnp.sum(raw_embed * raw_embed, axis=1, keepdims=True)) + norm_eps)
    unit_embed = raw_embed * inv_norm
    return (unit_embed, (patches, pre_stem, hidden, pre_mix, mixed, pooled, unit_embed, inv_norm))

def backward(feature_vector_derivative, saved, w_mix, w_out, w_proj):
    patches, pre_stem, hidden, pre_mix, mixed, pooled, unit_embed, inv_norm = saved
    number = pooled.shape[0]
    per_cutout = patches.shape[0] // number
    channels = hidden.shape[1]
    radial = lax.optimization_barrier(jnp.sum(unit_embed * feature_vector_derivative, axis=1, keepdims=True))
    grad_raw = (inv_norm * (feature_vector_derivative - unit_embed * radial)).astype(jnp.bfloat16)
    grad_proj = first_dot(pooled, grad_raw)
    grad_pool = (concluding_matrix_multiply(grad_raw, w_proj) / per_cutout).astype(jnp.bfloat16)
    mixed_sum = lax.optimization_barrier(jnp.sum(mixed.reshape(number, per_cutout, channels), axis=1, dtype=jnp.float32))
    grad_out = lax.dot_general(mixed_sum, grad_pool.astype(jnp.float32), (((0,), (0,)), ((), ())), precision=lax.Precision.HIGHEST, preferred_element_type=jnp.float32)
    grad_mixed = concluding_matrix_multiply(grad_pool, w_out)
    mix_slope = silu_slope(pre_mix).reshape(number, per_cutout, channels)
    grad_pre_mix = (grad_mixed[:, None, :] * mix_slope).reshape(-1, channels).astype(jnp.bfloat16)
    grad_mix = first_dot(hidden, grad_pre_mix)
    spread_pool = jnp.broadcast_to(grad_pool.astype(jnp.float32)[:, None, :], (number, per_cutout, channels)).reshape(-1, channels)
    grad_hidden = spread_pool + concluding_matrix_multiply(grad_pre_mix, w_mix)
    grad_pre_stem = (grad_hidden * silu_slope(pre_stem)).astype(jnp.bfloat16)
    grad_stem = first_dot(patches, grad_pre_stem)
    return (grad_stem, grad_mix, grad_out, grad_proj)

def contrast(anchor_feature_matrix, whole_feature_matrix, self_pos, pair_pos):
    cosine_affinity_matrix = concluding_matrix_multiply(anchor_feature_matrix, whole_feature_matrix) / logit_divisor_factor
    columns = lax.broadcasted_iota(jnp.int32, cosine_affinity_matrix.shape, 1)
    exp_scores = jnp.where(columns == self_pos[:, None], 0.0, jnp.exp(cosine_affinity_matrix))
    log_total = jnp.log(lax.optimization_barrier(jnp.sum(exp_scores, axis=1)))
    companion_feature_vector = jnp.take(whole_feature_matrix, pair_pos, axis=0).astype(jnp.float32)
    positive_couple_affinity = lax.optimization_barrier(jnp.sum(anchor_feature_matrix.astype(jnp.float32) * companion_feature_vector, axis=1)) / logit_divisor_factor
    return (exp_scores, log_total, companion_feature_vector, log_total - positive_couple_affinity)

def reference(cutouts, counts, partner, w_stem, w_mix, w_out, w_proj):
    node_rank = jnp.arange(NODE_DEV, dtype=jnp.int32)
    block_index = jnp.arange(N_VOL, dtype=jnp.int32)
    node_global = (node_rank[None, :] * N_VOL + block_index[:, None]).astype(jnp.int32)
    self_pos = (block_index[:, None] * NODE_DEV + node_rank[None, :]).astype(jnp.int32)
    grad_sums = (jnp.zeros(w_stem.shape, jnp.float32), jnp.zeros(w_mix.shape, jnp.float32), jnp.zeros(w_out.shape, jnp.float32), jnp.zeros(w_proj.shape, jnp.float32))
    losses = []
    for group in range(N_REP):
        group_counts = counts[group].astype(jnp.int32)
        inclusive = jnp.cumsum(group_counts).astype(jnp.int32)
        offsets = (inclusive - group_counts).astype(jnp.int32)
        owner = lax.optimization_barrier(jnp.sum((inclusive[None, None, :] <= node_global[:, :, None]).astype(jnp.int32), axis=2)).astype(jnp.int32)
        source = (owner * MAXN + node_global - jnp.take(offsets, owner)).astype(jnp.int32)
        group_cutouts = cutouts[group]

        def forward_block(carry, rows):
            unit_embed, saved = encode(jnp.take(group_cutouts, rows, axis=0), w_stem, w_mix, w_out, w_proj)
            return (carry, unit_embed.astype(jnp.bfloat16))
        _, blocks = lax.scan(forward_block, jnp.zeros((), jnp.float32), source)
        whole_feature_matrix = blocks.reshape(NODES, -1)
        pair_global = jnp.take(partner[group].astype(jnp.int32), node_global)
        pair_pos = (pair_global % N_VOL * NODE_DEV + pair_global // N_VOL).astype(jnp.int32)

        def total_block(carry, inputs):
            anchor_feature_matrix, self_rows, pair_rows = inputs
            _, log_total, _, row_loss = contrast(anchor_feature_matrix, whole_feature_matrix, self_rows, pair_rows)
            return (carry, (log_total, row_loss))
        _, (log_totals, group_loss) = lax.scan(total_block, jnp.zeros((), jnp.float32), (blocks, self_pos, pair_pos))
        all_totals = log_totals.reshape(NODES)

        def grad_block(carry, inputs):
            anchor_feature_matrix, self_rows, pair_rows, rows = inputs
            exp_scores, log_total, companion_feature_vector, _ = contrast(anchor_feature_matrix, whole_feature_matrix, self_rows, pair_rows)
            row_weight = (exp_scores * jnp.exp(-log_total)[:, None]).astype(jnp.bfloat16)
            column_weight = (exp_scores * jnp.exp(-all_totals)[None, :]).astype(jnp.bfloat16)
            horizontal_objective_term = jnp.dot(row_weight, whole_feature_matrix, preferred_element_type=jnp.float32)
            vertical_objective_term = jnp.dot(column_weight, whole_feature_matrix, preferred_element_type=jnp.float32)
            feature_vector_derivative = (horizontal_objective_term + vertical_objective_term - 2.0 * companion_feature_vector) / logit_divisor_factor
            _, saved = encode(jnp.take(group_cutouts, rows, axis=0), w_stem, w_mix, w_out, w_proj)
            grads = backward(feature_vector_derivative, saved, w_mix, w_out, w_proj)
            return (jax.tree.map(jnp.add, carry, grads), None)
        grad_sums, _ = lax.scan(grad_block, grad_sums, (blocks, self_pos, pair_pos, source))
        losses.append(group_loss)
    updates = [summed_grad * lax.rsqrt(jnp.mean(summed_grad * summed_grad) + rms_eps) for summed_grad in grad_sums]
    return (updates[0], updates[1], updates[2], updates[3], jnp.stack(losses))
```

```python
import jax
import jax.numpy as jnp
from jax import lax
from jax.experimental import pallas as pl
from jax.experimental.pallas import tpu as pltpu
from jax.sharding import PartitionSpec as P

TEMPERATURE = 0.2
NORM_EPS = 1e-06
RMS_EPS = 1e-06
BF16 = jnp.bfloat16
F32 = jnp.float32
GROUP = 4


def nn(left, right):
    return lax.dot_general(left, right, (((1,), (0,)), ((), ())), preferred_element_type=F32)


def nt(left, right):
    return lax.dot_general(left, right, (((1,), (1,)), ((), ())), preferred_element_type=F32)


def tn(left, right):
    return lax.dot_general(left, right, (((0,), (0,)), ((), ())), preferred_element_type=F32)


def sigmoid(value):
    return 0.5 + 0.5 * jnp.tanh(0.5 * value)


def split(value):
    high = value.astype(BF16)
    low = (value - high.astype(F32)).astype(BF16)
    return high, low


def paired(weight):
    zero = jnp.zeros_like(weight)
    return jnp.concatenate(
        [
            jnp.concatenate([weight, zero], axis=1),
            jnp.concatenate([zero, weight], axis=1),
        ],
        axis=0,
    )


def pair_rows(cut_ref, width, first, number):
    return jnp.concatenate(
        [cut_ref[:, (first + i) * width : (first + i + 1) * width] for i in range(number)], axis=0
    )


def forward_kernel(
    count_ref, cut_ref, stem_ref, mix_ref, out_ref, proj_ref,
    send_ref, pooled_ref, mixed_ref, unit_ref, inv_ref,
):
    nodes = cut_ref.shape[0]
    voxels, channels = stem_ref.shape
    width = 2 * voxels
    blocks = cut_ref.shape[1] // width
    stem2 = paired(stem_ref[...])
    mix2 = paired(mix_ref[...])
    hidden_sum = jnp.zeros((nodes, 2 * channels), F32)
    mixed_sum = jnp.zeros((nodes, 2 * channels), F32)
    for first in range(0, blocks, GROUP):
        number = min(GROUP, blocks - first)
        pre_stem = nn(pair_rows(cut_ref, width, first, number), stem2)
        hidden = (pre_stem * sigmoid(pre_stem)).astype(BF16)
        pre_mix = nn(hidden, mix2)
        mixed = (pre_mix * sigmoid(pre_mix)).astype(BF16)
        for i in range(number):
            rows = slice(i * nodes, (i + 1) * nodes)
            hidden_sum = hidden_sum + hidden[rows].astype(F32)
            mixed_sum = mixed_sum + mixed[rows].astype(F32)
    hidden_sum = hidden_sum[:, :channels] + hidden_sum[:, channels:]
    mixed_sum = mixed_sum[:, :channels] + mixed_sum[:, channels:]
    high, low = split(mixed_sum)
    weight = out_ref[...]
    summed = hidden_sum + (nn(high, weight) + nn(low, weight))
    pooled = (summed / (2 * blocks)).astype(BF16)
    raw = nn(pooled, proj_ref[...])
    inv = lax.rsqrt(jnp.sum(raw * raw, axis=1, keepdims=True) + NORM_EPS)
    unit = raw * inv
    count = count_ref[0]
    live = lax.broadcasted_iota(jnp.int32, unit.shape, 0) < count
    embed = jnp.where(live, unit, 0.0)
    counts = jnp.zeros(unit.shape, F32) + count.astype(F32)
    send_ref[...] = jnp.concatenate([embed, counts], axis=1).astype(BF16)
    pooled_ref[...] = pooled
    mixed_ref[...] = mixed_sum
    unit_ref[...] = unit
    inv_ref[...] = inv


def slope_kernel(
    send_ref, cut_ref, stem_ref, mix_ref, hidden_t_ref, patch_t_ref, stem_slope_ref, mix_slope_ref
):
    nodes = cut_ref.shape[0]
    voxels = stem_ref.shape[0]
    width = 2 * voxels
    blocks = cut_ref.shape[1] // width
    stem2 = paired(stem_ref[...])
    mix2 = paired(mix_ref[...])
    for first in range(0, blocks, GROUP):
        number = min(GROUP, blocks - first)
        rows = slice(first * nodes, (first + number) * nodes)
        patches = pair_rows(cut_ref, width, first, number)
        pre_stem = nn(patches, stem2)
        sigma = sigmoid(pre_stem)
        scaled = pre_stem * sigma
        hidden = scaled.astype(BF16)
        stem_slope_ref[rows, :] = sigma + scaled * (1.0 - sigma)
        pre_mix = nn(hidden, mix2)
        sigma = sigmoid(pre_mix)
        mix_slope_ref[rows, :] = sigma + pre_mix * sigma * (1.0 - sigma)
        hidden_t_ref[:, rows] = hidden.T
        patch_t_ref[:, rows] = patches.T


def slot_tables(gathered_ref, embed_dim, max_nodes):
    slots = gathered_ref.shape[0]
    owners = slots // max_nodes
    lane = lax.broadcasted_iota(jnp.int32, (8, gathered_ref.shape[1]), 1)
    pick = jnp.where(lane == embed_dim, 1.0, 0.0).astype(BF16)
    count = nt(pick, gathered_ref[...])
    slot = lax.broadcasted_iota(jnp.int32, (8, slots), 1)
    heads = jnp.where(slot % max_nodes == 0, count, 0.0)
    step = min(slots, 512)
    row = lax.broadcasted_iota(jnp.int32, (step, slots), 0)
    column_owner = lax.broadcasted_iota(jnp.int32, (step, slots), 1) // max_nodes
    offset = jnp.zeros((8, slots), F32)
    for first in range(0, slots, step):
        earlier = jnp.where((row + first) // max_nodes < column_owner, 1.0, 0.0).astype(BF16)
        offset = offset + nn(heads[:, first : first + step].astype(BF16), earlier)
    del owners
    return count[0:1], offset[0:1], heads[0:1]


def score_sums(gathered_ref, embed_dim, max_nodes, live_row):
    slots = gathered_ref.shape[0]
    step = min(slots, 256)
    whole = gathered_ref[:, :embed_dim]

    def block(first, total):
        part = gathered_ref[pl.ds(first, step), :]
        scores = nt(part[:, :embed_dim], whole) / TEMPERATURE
        count = part[:, embed_dim : embed_dim + 1].astype(F32)
        row = lax.broadcasted_iota(jnp.int32, (step, 1), 0) + first
        live = (row % max_nodes).astype(F32) < count
        column = lax.broadcasted_iota(jnp.int32, scores.shape, 1)
        keep = jnp.logical_and(live, column != row)
        return total + jnp.sum(jnp.where(keep, jnp.exp(scores), 0.0), axis=0, keepdims=True)

    total = jnp.zeros((1, slots), F32)
    if slots == step:
        total = block(0, total)
    else:
        total = lax.fori_loop(
            0, slots // step, lambda i, t: block(pl.multiple_of(i * step, step), t), total
        )
    return jnp.where(live_row, total, 1.0)


def backward_kernel(
    place_ref, gathered_ref, partner_ref, send_ref, pooled_ref, mixed_ref, unit_ref, inv_ref,
    hidden_t_ref, patch_t_ref, stem_slope_ref, mix_slope_ref, mix_ref, out_ref, proj_ref, grad_ref,
):
    nodes, embed_dim = unit_ref.shape
    slots = gathered_ref.shape[0]
    place = place_ref[0]
    own_count = place_ref[1]
    channels = mix_ref.shape[0]
    voxels = patch_t_ref.shape[0] // 2
    blocks = stem_slope_ref.shape[0] // nodes

    count_row, offset_row, heads = slot_tables(gathered_ref, embed_dim, nodes)
    slot_row = lax.broadcasted_iota(jnp.int32, (1, slots), 1)
    within = (slot_row % nodes).astype(F32)
    live_row = within < count_row
    number_row = jnp.where(live_row, offset_row + within, -1.0)
    totals = score_sums(gathered_ref, embed_dim, nodes, live_row)

    own_offset = jnp.sum(
        jnp.where(slot_row // nodes < place, heads, 0.0), axis=1, keepdims=True
    )
    rank = lax.broadcasted_iota(jnp.int32, (nodes, 1), 0)
    own_live = rank < own_count
    own_number = own_offset + rank.astype(F32)
    partner = partner_ref[...].astype(F32)
    listed = lax.broadcasted_iota(jnp.int32, (nodes, partner.shape[1]), 1).astype(F32)
    mate = jnp.sum(jnp.where(listed == own_number, partner, 0.0), axis=1, keepdims=True)
    companion = jnp.where(number_row == mate, 1.0, 0.0).astype(BF16)

    whole = gathered_ref[:, :embed_dim]
    scores = nt(send_ref[:, :embed_dim], whole) / TEMPERATURE
    other = jnp.logical_and(live_row, slot_row != rank + place * nodes)
    weight = jnp.where(other, jnp.exp(scores), 0.0)
    own_total = jnp.sum(weight, axis=1, keepdims=True)
    row_weight = (weight * (1.0 / own_total)).astype(BF16)
    column_weight = (weight * (1.0 / totals)).astype(BF16)
    mixed_rows = nn(jnp.concatenate([row_weight, column_weight, companion], axis=0), whole)
    d_embed = (
        mixed_rows[:nodes] + mixed_rows[nodes : 2 * nodes] - 2.0 * mixed_rows[2 * nodes :]
    ) / TEMPERATURE

    unit = unit_ref[...]
    radial = jnp.sum(unit * d_embed, axis=1, keepdims=True)
    d_raw = jnp.where(own_live, inv_ref[...] * (d_embed - unit * radial), 0.0).astype(BF16)
    g_proj = tn(pooled_ref[...], d_raw)
    d_sum = (nt(d_raw, proj_ref[...]) / (2 * blocks)).astype(BF16)
    high, low = split(mixed_ref[...])
    g_out = tn(high, d_sum) + tn(low, d_sum)
    d_mixed = nt(d_sum, out_ref[...])
    d_mixed = jnp.concatenate([d_mixed, d_mixed], axis=1)
    d_pool = d_sum.astype(F32)
    d_pool = jnp.concatenate([d_pool, d_pool], axis=1)
    mix2 = paired(mix_ref[...])

    g_mix = jnp.zeros((2 * channels, 2 * channels), F32)
    g_stem = jnp.zeros((2 * voxels, 2 * channels), F32)
    chunk = 2 * GROUP
    for first in range(0, blocks, chunk):
        number = min(chunk, blocks - first)
        rows = slice(first * nodes, (first + number) * nodes)
        d_pre_mix = jnp.concatenate(
            [
                (d_mixed * mix_slope_ref[(first + i) * nodes : (first + i + 1) * nodes, :]).astype(BF16)
                for i in range(number)
            ],
            axis=0,
        )
        g_mix = g_mix + nn(hidden_t_ref[:, rows], d_pre_mix)
        back = nt(d_pre_mix, mix2)
        d_pre_stem = jnp.concatenate(
            [
                (
                    (d_pool + back[i * nodes : (i + 1) * nodes])
                    * stem_slope_ref[(first + i) * nodes : (first + i + 1) * nodes, :]
                ).astype(BF16)
                for i in range(number)
            ],
            axis=0,
        )
        g_stem = g_stem + nn(patch_t_ref[:, rows], d_pre_stem)
    g_mix = g_mix[:channels, :channels] + g_mix[channels:, channels:]
    g_stem = g_stem[:voxels, :channels] + g_stem[voxels:, channels:]
    half = channels // 2
    g_proj = jnp.concatenate([g_proj[:half], g_proj[half:]], axis=1)
    grad_ref[...] = jnp.concatenate([g_stem, g_mix, g_out, g_proj], axis=0).astype(grad_ref.dtype)


def loss_kernel(place_ref, gathered_ref, partner_ref, anchor_ref, loss_ref, *, embed_dim, max_nodes):
    slots = gathered_ref.shape[0]
    owners = slots // max_nodes
    place = place_ref[0]
    node_dev = loss_ref.shape[0]
    del anchor_ref
    count_row, offset_row, _ = slot_tables(gathered_ref, embed_dim, max_nodes)
    slot_row = lax.broadcasted_iota(jnp.int32, (1, slots), 1)
    within = (slot_row % max_nodes).astype(F32)
    live_row = within < count_row
    number_row = jnp.where(live_row, offset_row + within, -1.0)
    totals = score_sums(gathered_ref, embed_dim, max_nodes, live_row)
    number = (lax.broadcasted_iota(jnp.int32, (node_dev, 1), 0) * owners + place).astype(F32)
    partner = partner_ref[...].astype(F32)
    listed = lax.broadcasted_iota(jnp.int32, (node_dev, partner.shape[1]), 1).astype(F32)
    mate = jnp.sum(jnp.where(listed == number, partner, 0.0), axis=1, keepdims=True)
    mine = number_row == number
    total = jnp.sum(jnp.where(mine, totals, 0.0), axis=1, keepdims=True)
    whole = gathered_ref[:, :embed_dim]
    anchor = nn(jnp.where(mine, 1.0, 0.0).astype(BF16), whole)
    companion = nn(jnp.where(number_row == mate, 1.0, 0.0).astype(BF16), whole)
    positive = jnp.sum(anchor * companion, axis=1, keepdims=True) / TEMPERATURE
    loss_ref[...] = jnp.broadcast_to(jnp.log(total) - positive, loss_ref.shape)


def update_kernel(grad_ref, stem_ref, mix_ref, out_ref, proj_ref):
    start = 0
    for ref in (stem_ref, mix_ref, out_ref, proj_ref):
        size = ref.shape[0] * ref.shape[1]
        rows = size // grad_ref.shape[1]
        grad = grad_ref[start : start + rows, :].astype(F32)
        start += rows
        squares = jnp.sum(jnp.sum(grad * grad, axis=0, keepdims=True), axis=1, keepdims=True)
        update = grad * lax.rsqrt(squares / size + RMS_EPS)
        if ref.shape[1] == grad_ref.shape[1]:
            ref[...] = update
        else:
            half = ref.shape[1]
            ref[:rows, :] = update[:, :half]
            ref[rows:, :] = update[:, half:]


def vmem(number):
    return [pl.BlockSpec(memory_space=pltpu.VMEM)] * number


def smem():
    return pl.BlockSpec(memory_space=pltpu.SMEM)


def on_device(cutouts, counts, partner, w_stem, w_mix, w_out, w_proj):
    axes = ("vol", "rep")
    owners = lax.axis_size("vol")
    devices = owners * lax.axis_size("rep")
    place = lax.axis_index("vol").astype(jnp.int32)
    cut = cutouts[0]
    nodes = cut.shape[0]
    voxels, channels = w_stem.shape
    embed_dim = w_proj.shape[1]
    rows = cut.shape[1] // (2 * voxels) * nodes
    own_count = counts[0]
    shape = jax.ShapeDtypeStruct

    send, pooled, mixed_sum, unit, inv = pl.pallas_call(
        forward_kernel,
        out_shape=(
            shape((nodes, 2 * embed_dim), BF16),
            shape((nodes, channels), BF16),
            shape((nodes, channels), F32),
            shape((nodes, embed_dim), F32),
            shape((nodes, 1), F32),
        ),
        in_specs=[smem()] + vmem(5),
        out_specs=tuple(vmem(5)),
    )(own_count, cut, w_stem, w_mix, w_out, w_proj)

    gathered = lax.all_to_all(
        jnp.broadcast_to(send[None], (owners,) + send.shape), "vol", 0, 0
    ).reshape(owners * nodes, 2 * embed_dim)

    hidden_t, patch_t, stem_slope, mix_slope = pl.pallas_call(
        slope_kernel,
        out_shape=(
            shape((2 * channels, rows), BF16),
            shape((2 * voxels, rows), BF16),
            shape((rows, 2 * channels), F32),
            shape((rows, 2 * channels), F32),
        ),
        in_specs=vmem(4),
        out_specs=tuple(vmem(4)),
    )(send, cut, w_stem, w_mix)

    where = jnp.stack([place, own_count[0]])
    total_rows = (w_stem.size + w_mix.size + w_out.size + w_proj.size) // channels
    grad = pl.pallas_call(
        backward_kernel,
        out_shape=shape((total_rows, channels), BF16),
        in_specs=[smem()] + vmem(14),
        out_specs=vmem(1)[0],
    )(
        where, gathered, partner, send, pooled, mixed_sum, unit, inv,
        hidden_t, patch_t, stem_slope, mix_slope, w_mix, w_out, w_proj,
    )

    share = (total_rows + devices - 1) // devices
    if share * devices != total_rows:
        grad = jnp.pad(grad, ((0, share * devices - total_rows), (0, 0)))
    parts = lax.all_to_all(grad.reshape(devices, share, channels), axes, 0, 0)
    mine = jnp.sum(parts.astype(F32), axis=0).astype(BF16)
    whole = lax.all_to_all(jnp.broadcast_to(mine[None], (devices,) + mine.shape), axes, 0, 0)
    whole = whole.reshape(devices * share, channels)[:total_rows]

    node_dev = partner.shape[1] // owners
    loss = pl.pallas_call(
        lambda *refs: loss_kernel(*refs, embed_dim=embed_dim, max_nodes=nodes),
        out_shape=shape((node_dev, 128), F32),
        in_specs=[smem()] + vmem(2) + [pl.BlockSpec(memory_space=pl.ANY)],
        out_specs=vmem(1)[0],
    )(where, gathered, partner, grad)

    updates = pl.pallas_call(
        update_kernel,
        out_shape=tuple(shape(w.shape, F32) for w in (w_stem, w_mix, w_out, w_proj)),
        in_specs=vmem(1),
        out_specs=tuple(vmem(4)),
    )(whole)
    return (*updates, loss[:, 0][None, None, :])


def solution(mesh):
    in_specs = (P("rep", "vol", None), P("rep", "vol"), P("rep", None), P(), P(), P(), P())
    out_specs = (P(), P(), P(), P(), P("rep", "vol", None))
    return jax.shard_map(
        on_device, mesh=mesh, in_specs=in_specs, out_specs=out_specs, check_vma=False
    )
```

```python
import jax
import jax.numpy as jnp
from jax import lax
from jax.experimental import pallas as pl
from jax.experimental.pallas import tpu as pltpu
from jax.sharding import PartitionSpec as P

TEMPERATURE = 0.2
NORM_EPS = 1e-06
RMS_EPS = 1e-06
BF16 = jnp.bfloat16
F32 = jnp.float32
GROUP = 4


def nn(left, right):
    return lax.dot_general(left, right, (((1,), (0,)), ((), ())), preferred_element_type=F32)


def nt(left, right):
    return lax.dot_general(left, right, (((1,), (1,)), ((), ())), preferred_element_type=F32)


def tn(left, right):
    return lax.dot_general(left, right, (((0,), (0,)), ((), ())), preferred_element_type=F32)


def sigmoid(value):
    return 0.5 + 0.5 * jnp.tanh(0.5 * value)


def split(value):
    high = value.astype(BF16)
    low = (value - high.astype(F32)).astype(BF16)
    return high, low


def paired(weight):
    zero = jnp.zeros_like(weight)
    return jnp.concatenate(
        [
            jnp.concatenate([weight, zero], axis=1),
            jnp.concatenate([zero, weight], axis=1),
        ],
        axis=0,
    )


def pair_rows(cut_ref, width, first, number):
    return jnp.concatenate(
        [cut_ref[:, (first + i) * width : (first + i + 1) * width] for i in range(number)], axis=0
    )


def forward_kernel(
    count_ref, cut_ref, stem_ref, mix_ref, out_ref, proj_ref,
    send_ref, pooled_ref, mixed_ref, unit_ref, inv_ref,
):
    nodes = cut_ref.shape[0]
    voxels, channels = stem_ref.shape
    width = 2 * voxels
    blocks = cut_ref.shape[1] // width
    stem2 = paired(stem_ref[...])
    mix2 = paired(mix_ref[...])
    hidden_sum = jnp.zeros((nodes, 2 * channels), F32)
    mixed_sum = jnp.zeros((nodes, 2 * channels), F32)
    for first in range(0, blocks, GROUP):
        number = min(GROUP, blocks - first)
        pre_stem = nn(pair_rows(cut_ref, width, first, number), stem2)
        hidden = (pre_stem * sigmoid(pre_stem)).astype(BF16)
        pre_mix = nn(hidden, mix2)
        mixed = (pre_mix * sigmoid(pre_mix)).astype(BF16)
        for i in range(number):
            rows = slice(i * nodes, (i + 1) * nodes)
            hidden_sum = hidden_sum + hidden[rows].astype(F32)
            mixed_sum = mixed_sum + mixed[rows].astype(F32)
    hidden_sum = hidden_sum[:, :channels] + hidden_sum[:, channels:]
    mixed_sum = mixed_sum[:, :channels] + mixed_sum[:, channels:]
    high, low = split(mixed_sum)
    weight = out_ref[...]
    summed = hidden_sum + (nn(high, weight) + nn(low, weight))
    pooled = (summed / (2 * blocks)).astype(BF16)
    raw = nt(pooled, proj_ref[...])
    inv = lax.rsqrt(jnp.sum(raw * raw, axis=1, keepdims=True) + NORM_EPS)
    unit = raw * inv
    count = count_ref[...]
    live = lax.broadcasted_iota(jnp.int32, unit.shape, 0) < count
    embed = jnp.where(live, unit, 0.0)
    counts = jnp.zeros(unit.shape, F32) + count.astype(F32)
    send = jnp.concatenate([embed, counts], axis=1).astype(BF16)
    send_ref[...] = jnp.broadcast_to(send[None], send_ref.shape)
    pooled_ref[...] = pooled
    mixed_ref[...] = mixed_sum
    unit_ref[...] = unit
    inv_ref[...] = inv


def slope_kernel(
    send_ref, cut_ref, stem_ref, mix_ref, hidden_t_ref, patch_t_ref, stem_slope_ref, mix_slope_ref
):
    del send_ref
    nodes = cut_ref.shape[0]
    voxels = stem_ref.shape[0]
    width = 2 * voxels
    blocks = cut_ref.shape[1] // width
    stem2 = paired(stem_ref[...])
    mix2 = paired(mix_ref[...])
    for first in range(0, blocks, GROUP):
        number = min(GROUP, blocks - first)
        rows = slice(first * nodes, (first + number) * nodes)
        patches = pair_rows(cut_ref, width, first, number)
        pre_stem = nn(patches, stem2)
        sigma = sigmoid(pre_stem)
        scaled = pre_stem * sigma
        hidden = scaled.astype(BF16)
        stem_slope_ref[rows, :] = sigma + scaled * (1.0 - sigma)
        pre_mix = nn(hidden, mix2)
        sigma = sigmoid(pre_mix)
        mix_slope_ref[rows, :] = sigma + pre_mix * sigma * (1.0 - sigma)
        hidden_t_ref[:, rows] = hidden.T
        patch_t_ref[:, rows] = patches.T


def slot_tables(gathered_ref, embed_dim, max_nodes):
    slots = gathered_ref.shape[0]
    owners = slots // max_nodes
    lane = lax.broadcasted_iota(jnp.int32, (8, gathered_ref.shape[1]), 1)
    pick = jnp.where(lane == embed_dim, 1.0, 0.0).astype(BF16)
    count = nt(pick, gathered_ref[...])
    slot = lax.broadcasted_iota(jnp.int32, (8, slots), 1)
    heads = jnp.where(slot % max_nodes == 0, count, 0.0)
    step = min(slots, 512)
    row = lax.broadcasted_iota(jnp.int32, (step, slots), 0)
    column_owner = lax.broadcasted_iota(jnp.int32, (step, slots), 1) // max_nodes
    offset = jnp.zeros((8, slots), F32)
    for first in range(0, slots, step):
        earlier = jnp.where((row + first) // max_nodes < column_owner, 1.0, 0.0).astype(BF16)
        offset = offset + nn(heads[:, first : first + step].astype(BF16), earlier)
    del owners
    return count[0:1], offset[0:1], heads[0:1]


def score_sums(gathered_ref, embed_dim, max_nodes, live_row):
    slots = gathered_ref.shape[0]
    step = min(slots, 256)
    whole = gathered_ref[:, :embed_dim]

    def block(first, total):
        part = gathered_ref[pl.ds(first, step), :]
        scores = nt(part[:, :embed_dim], whole) / TEMPERATURE
        count = part[:, embed_dim : embed_dim + 1].astype(F32)
        row = lax.broadcasted_iota(jnp.int32, (step, 1), 0) + first
        live = (row % max_nodes).astype(F32) < count
        column = lax.broadcasted_iota(jnp.int32, scores.shape, 1)
        keep = jnp.logical_and(live, column != row)
        return total + jnp.sum(jnp.where(keep, jnp.exp(scores), 0.0), axis=0, keepdims=True)

    total = jnp.zeros((1, slots), F32)
    if slots == step:
        total = block(0, total)
    else:
        total = lax.fori_loop(
            0, slots // step, lambda i, t: block(pl.multiple_of(i * step, step), t), total
        )
    return jnp.where(live_row, total, 1.0)


def backward_kernel(
    count_ref, gathered_ref, partner_ref, pooled_ref, mixed_ref, unit_ref, inv_ref,
    hidden_t_ref, patch_t_ref, stem_slope_ref, mix_slope_ref, mix_ref, out_ref, proj_ref, grad_ref,
):
    nodes, embed_dim = unit_ref.shape
    slots = gathered_ref.shape[0]
    place = lax.axis_index("vol")
    own_count = count_ref[...]
    channels = mix_ref.shape[0]
    voxels = patch_t_ref.shape[0] // 2
    blocks = stem_slope_ref.shape[0] // nodes

    count_row, offset_row, heads = slot_tables(gathered_ref, embed_dim, nodes)
    slot_row = lax.broadcasted_iota(jnp.int32, (1, slots), 1)
    within = (slot_row % nodes).astype(F32)
    live_row = within < count_row
    number_row = jnp.where(live_row, offset_row + within, -1.0)
    totals = score_sums(gathered_ref, embed_dim, nodes, live_row)

    own_offset = jnp.sum(
        jnp.where(slot_row // nodes < place, heads, 0.0), axis=1, keepdims=True
    )
    rank = lax.broadcasted_iota(jnp.int32, (nodes, 1), 0)
    own_live = rank < own_count
    own_number = own_offset + rank.astype(F32)
    partner = partner_ref[...].astype(F32)
    listed = lax.broadcasted_iota(jnp.int32, (nodes, partner.shape[1]), 1).astype(F32)
    mate = jnp.sum(jnp.where(listed == own_number, partner, 0.0), axis=1, keepdims=True)
    companion = jnp.where(number_row == mate, 1.0, 0.0).astype(BF16)

    whole = gathered_ref[:, :embed_dim]
    own = gathered_ref[pl.ds(pl.multiple_of(place * nodes, nodes), nodes), :]
    scores = nt(own[:, :embed_dim], whole) / TEMPERATURE
    other = jnp.logical_and(live_row, slot_row != rank + place * nodes)
    weight = jnp.where(other, jnp.exp(scores), 0.0)
    own_total = jnp.sum(weight, axis=1, keepdims=True)
    row_weight = (weight * (1.0 / own_total)).astype(BF16)
    column_weight = (weight * (1.0 / totals)).astype(BF16)
    mixed_rows = nn(jnp.concatenate([row_weight, column_weight, companion], axis=0), whole)
    d_embed = (
        mixed_rows[:nodes] + mixed_rows[nodes : 2 * nodes] - 2.0 * mixed_rows[2 * nodes :]
    ) / TEMPERATURE

    unit = unit_ref[...]
    radial = jnp.sum(unit * d_embed, axis=1, keepdims=True)
    d_raw = jnp.where(own_live, inv_ref[...] * (d_embed - unit * radial), 0.0).astype(BF16)
    g_proj = tn(d_raw, pooled_ref[...])
    d_sum = (nn(d_raw, proj_ref[...]) / (2 * blocks)).astype(BF16)
    high, low = split(mixed_ref[...])
    g_out = tn(high, d_sum) + tn(low, d_sum)
    d_mixed = nt(d_sum, out_ref[...])
    d_mixed = jnp.concatenate([d_mixed, d_mixed], axis=1)
    d_pool = d_sum.astype(F32)
    d_pool = jnp.concatenate([d_pool, d_pool], axis=1)
    mix2 = paired(mix_ref[...])

    g_mix = jnp.zeros((2 * channels, 2 * channels), F32)
    g_stem = jnp.zeros((2 * voxels, 2 * channels), F32)
    chunk = 2 * GROUP
    for first in range(0, blocks, chunk):
        number = min(chunk, blocks - first)
        rows = slice(first * nodes, (first + number) * nodes)
        d_pre_mix = jnp.concatenate(
            [
                (d_mixed * mix_slope_ref[(first + i) * nodes : (first + i + 1) * nodes, :]).astype(BF16)
                for i in range(number)
            ],
            axis=0,
        )
        g_mix = g_mix + nn(hidden_t_ref[:, rows], d_pre_mix)
        back = nt(d_pre_mix, mix2)
        d_pre_stem = jnp.concatenate(
            [
                (
                    (d_pool + back[i * nodes : (i + 1) * nodes])
                    * stem_slope_ref[(first + i) * nodes : (first + i + 1) * nodes, :]
                ).astype(BF16)
                for i in range(number)
            ],
            axis=0,
        )
        g_stem = g_stem + nn(patch_t_ref[:, rows], d_pre_stem)
    g_mix = g_mix[:channels, :channels] + g_mix[channels:, channels:]
    g_stem = g_stem[:voxels, :channels] + g_stem[voxels:, channels:]
    pack(grad_ref, jnp.concatenate([g_stem, g_mix, g_out, g_proj], axis=0))


def pack(ref, value):
    if len(ref.shape) == 2:
        ref[...] = value.astype(ref.dtype)
        return
    devices, share, width = ref.shape
    full = share // 8 * 8
    rest = share - full
    head = value[: devices * full].reshape(devices, full, width)
    ref[:, :full, :] = head.astype(ref.dtype)
    if rest:
        tail = value[devices * full :].reshape(devices, rest, width)
        ref[:, full:, :] = tail.astype(ref.dtype)


def unpack(ref):
    if len(ref.shape) == 2:
        return ref[...].astype(F32)
    devices, share, width = ref.shape
    full = share // 8 * 8
    rest = share - full
    value = ref[:, :full, :].astype(F32).reshape(devices * full, width)
    if rest:
        tail = ref[:, full:, :].astype(F32).reshape(devices * rest, width)
        value = jnp.concatenate([value, tail], axis=0)
    return value


def loss_kernel(after_ref, gathered_ref, partner_ref, loss_ref, *, embed_dim, max_nodes):
    del after_ref
    slots = gathered_ref.shape[0]
    owners = slots // max_nodes
    place = lax.axis_index("vol")
    node_dev = loss_ref.shape[1]
    count_row, offset_row, _ = slot_tables(gathered_ref, embed_dim, max_nodes)
    slot_row = lax.broadcasted_iota(jnp.int32, (1, slots), 1)
    within = (slot_row % max_nodes).astype(F32)
    live_row = within < count_row
    number_row = jnp.where(live_row, offset_row + within, -1.0)
    totals = score_sums(gathered_ref, embed_dim, max_nodes, live_row)
    number = (lax.broadcasted_iota(jnp.int32, (node_dev, 1), 0) * owners + place).astype(F32)
    partner = partner_ref[...].astype(F32)
    listed = lax.broadcasted_iota(jnp.int32, (node_dev, partner.shape[1]), 1).astype(F32)
    mate = jnp.sum(jnp.where(listed == number, partner, 0.0), axis=1, keepdims=True)
    mine = number_row == number
    total = jnp.sum(jnp.where(mine, totals, 0.0), axis=1, keepdims=True)
    whole = gathered_ref[:, :embed_dim]
    anchor = nn(jnp.where(mine, 1.0, 0.0).astype(BF16), whole)
    companion = nn(jnp.where(number_row == mate, 1.0, 0.0).astype(BF16), whole)
    positive = jnp.sum(anchor * companion, axis=1, keepdims=True) / TEMPERATURE
    loss = jnp.log(total) - positive
    row = lax.broadcasted_iota(jnp.int32, (node_dev, node_dev), 0)
    column = lax.broadcasted_iota(jnp.int32, (node_dev, node_dev), 1)
    loss_ref[...] = jnp.sum(jnp.where(row == column, loss, 0.0), axis=0, keepdims=True)


def share_kernel(part_ref, send_ref):
    total = jnp.sum(part_ref[...].astype(F32), axis=0, keepdims=True).astype(send_ref.dtype)
    send_ref[...] = jnp.broadcast_to(total, send_ref.shape)


def update_kernel(grad_ref, *refs):
    value = unpack(grad_ref)
    start = 0
    for ref in refs:
        rows = ref.shape[0]
        grad = value[start : start + rows]
        start += rows
        squares = jnp.sum(jnp.sum(grad * grad, axis=0, keepdims=True), axis=1, keepdims=True)
        ref[...] = grad * lax.rsqrt(squares / (rows * ref.shape[1]) + RMS_EPS)


def vmem(number):
    return [pl.BlockSpec(memory_space=pltpu.VMEM)] * number


def anywhere():
    return pl.BlockSpec(memory_space=pl.ANY)


def on_device(cutouts, counts, partner, w_stem, w_mix, w_out, w_proj):
    axes = ("vol", "rep")
    owners = lax.axis_size("vol")
    devices = owners * lax.axis_size("rep")
    cut = cutouts[0]
    nodes = cut.shape[0]
    voxels, channels = w_stem.shape
    embed_dim = w_proj.shape[1]
    rows = cut.shape[1] // (2 * voxels) * nodes
    w_proj = w_proj.T
    shape = jax.ShapeDtypeStruct
    params = pltpu.CompilerParams(vmem_limit_bytes=(16 << 20) + owners * nodes * 8192)

    send, pooled, mixed_sum, unit, inv = pl.pallas_call(
        forward_kernel,
        out_shape=(
            shape((owners, nodes, 2 * embed_dim), BF16),
            shape((nodes, channels), BF16),
            shape((nodes, channels), F32),
            shape((nodes, embed_dim), F32),
            shape((nodes, 1), F32),
        ),
        in_specs=vmem(6),
        out_specs=tuple(vmem(5)),
        compiler_params=params,
        name="forward",
    )(counts, cut, w_stem, w_mix, w_out, w_proj)

    gathered = lax.all_to_all(send, "vol", 0, 0).reshape(owners * nodes, 2 * embed_dim)

    hidden_t, patch_t, stem_slope, mix_slope = pl.pallas_call(
        slope_kernel,
        out_shape=(
            shape((2 * channels, rows), BF16),
            shape((2 * voxels, rows), BF16),
            shape((rows, 2 * channels), F32),
            shape((rows, 2 * channels), F32),
        ),
        in_specs=[anywhere()] + vmem(3),
        out_specs=tuple(vmem(4)),
        compiler_params=params,
        name="slopes",
    )(pooled, cut, w_stem, w_mix)

    weights = (w_stem, w_mix, w_out, w_proj)
    total_rows = sum(w.shape[0] for w in weights)
    share = (total_rows + devices - 1) // devices
    packed = share * devices == total_rows and share >= 8 and share % 4 == 0
    grad = pl.pallas_call(
        backward_kernel,
        out_shape=shape((devices, share, channels) if packed else (total_rows, channels), BF16),
        in_specs=vmem(14),
        out_specs=vmem(1)[0],
        compiler_params=params,
        name="backward",
    )(
        counts, gathered, partner, pooled, mixed_sum, unit, inv,
        hidden_t, patch_t, stem_slope, mix_slope, w_mix, w_out, w_proj,
    )

    parts = grad
    if not packed:
        parts = jnp.pad(grad, ((0, share * devices - total_rows), (0, 0)))
        parts = parts.reshape(devices, share, channels)
    parts = lax.all_to_all(parts, axes, 0, 0)
    whole = pl.pallas_call(
        share_kernel,
        out_shape=shape(parts.shape, BF16),
        in_specs=vmem(1),
        out_specs=vmem(1)[0],
        compiler_params=params,
        name="share",
    )(parts)
    whole = lax.all_to_all(whole, axes, 0, 0)
    if not packed:
        whole = whole.reshape(devices * share, channels)[:total_rows]

    node_dev = partner.shape[1] // owners
    loss = pl.pallas_call(
        lambda *refs: loss_kernel(*refs, embed_dim=embed_dim, max_nodes=nodes),
        out_shape=shape((1, node_dev), F32),
        in_specs=[anywhere()] + vmem(2),
        out_specs=vmem(1)[0],
        compiler_params=params,
        name="losses",
    )(grad, gathered, partner)

    updates = pl.pallas_call(
        update_kernel,
        out_shape=tuple(shape(w.shape, F32) for w in weights),
        in_specs=vmem(1),
        out_specs=tuple(vmem(4)),
        compiler_params=params,
        name="updates",
    )(whole)
    return (*updates[:3], updates[3].T, loss[None])


def solution(mesh):
    in_specs = (P("rep", "vol", None), P("rep", "vol"), P("rep", None), P(), P(), P(), P())
    out_specs = (P(), P(), P(), P(), P("rep", "vol", None))
    return jax.shard_map(
        on_device, mesh=mesh, in_specs=in_specs, out_specs=out_specs, check_vma=False
    )
```

```python
import jax
import jax.numpy as jnp
from jax import lax
from jax.experimental import pallas as pl
from jax.experimental.pallas import tpu as pltpu
from jax.sharding import PartitionSpec as P

TEMPERATURE = 0.2
NORM_EPS = 1e-06
RMS_EPS = 1e-06
BF16 = jnp.bfloat16
F32 = jnp.float32
GROUP = 4


def nn(left, right):
    return lax.dot_general(left, right, (((1,), (0,)), ((), ())), preferred_element_type=F32)


def nt(left, right):
    return lax.dot_general(left, right, (((1,), (1,)), ((), ())), preferred_element_type=F32)


def tn(left, right):
    return lax.dot_general(left, right, (((0,), (0,)), ((), ())), preferred_element_type=F32)


def sigmoid(value):
    return 0.5 + 0.5 * jnp.tanh(0.5 * value)


def split(value):
    high = value.astype(BF16)
    low = (value - high.astype(F32)).astype(BF16)
    return high, low


def paired(weight):
    zero = jnp.zeros_like(weight)
    return jnp.concatenate(
        [
            jnp.concatenate([weight, zero], axis=1),
            jnp.concatenate([zero, weight], axis=1),
        ],
        axis=0,
    )


def pair_rows(cut_ref, width, first, number):
    return jnp.concatenate(
        [cut_ref[:, (first + i) * width : (first + i + 1) * width] for i in range(number)], axis=0
    )


def forward_kernel(
    count_ref, cut_hbm, stem_hbm, mix_hbm, out_hbm, proj_hbm,
    send_ref, pooled_ref, mixed_ref, unit_ref, inv_ref,
    cut_ref, stem_ref, mix_ref, out_ref, proj_ref, sems, cut_sems,
):
    nodes = cut_ref.shape[0]
    voxels, channels = stem_ref.shape
    width = 2 * voxels
    blocks = cut_ref.shape[1] // width

    def cut_copy(first):
        lanes = pl.ds(first * width, min(GROUP, blocks - first) * width)
        return pltpu.make_async_copy(
            cut_hbm.at[:, lanes], cut_ref.at[:, lanes], cut_sems.at[first // GROUP]
        )

    def copy(index, source, target):
        return pltpu.make_async_copy(source, target, sems.at[index])

    stem_copy = copy(0, stem_hbm, stem_ref)
    mix_copy = copy(1, mix_hbm, mix_ref)
    late = (copy(2, out_hbm, out_ref), copy(3, proj_hbm, proj_ref))
    stem_copy.start()
    cut_copy(0).start()
    mix_copy.start()
    for first in range(GROUP, blocks, GROUP):
        cut_copy(first).start()
    for each in late:
        each.start()
    stem_copy.wait()
    stem2 = paired(stem_ref[...])
    mix2 = None
    hidden_sum = jnp.zeros((nodes, 2 * channels), F32)
    mixed_sum = jnp.zeros((nodes, 2 * channels), F32)
    for first in range(0, blocks, GROUP):
        number = min(GROUP, blocks - first)
        cut_copy(first).wait()
        pre_stem = nn(pair_rows(cut_ref, width, first, number), stem2)
        hidden = (pre_stem * sigmoid(pre_stem)).astype(BF16)
        if first == 0:
            mix_copy.wait()
            mix2 = paired(mix_ref[...])
        pre_mix = nn(hidden, mix2)
        mixed = (pre_mix * sigmoid(pre_mix)).astype(BF16)
        for i in range(number):
            rows = slice(i * nodes, (i + 1) * nodes)
            hidden_sum = hidden_sum + hidden[rows].astype(F32)
            mixed_sum = mixed_sum + mixed[rows].astype(F32)
    hidden_sum = hidden_sum[:, :channels] + hidden_sum[:, channels:]
    mixed_sum = mixed_sum[:, :channels] + mixed_sum[:, channels:]
    high, low = split(mixed_sum)
    for each in late:
        each.wait()
    weight = out_ref[...]
    summed = hidden_sum + (nn(high, weight) + nn(low, weight))
    pooled = (summed / (2 * blocks)).astype(BF16)
    raw = nt(pooled, proj_ref[...])
    inv = lax.rsqrt(jnp.sum(raw * raw, axis=1, keepdims=True) + NORM_EPS)
    unit = raw * inv
    count = count_ref[0, 0]
    live = lax.broadcasted_iota(jnp.int32, unit.shape, 0) < count
    embed = jnp.where(live, unit, 0.0)
    counts = jnp.zeros(unit.shape, F32) + count.astype(F32)
    send = jnp.concatenate([embed, counts], axis=1).astype(BF16)
    send_ref[...] = jnp.broadcast_to(send[None], send_ref.shape)
    pooled_ref[...] = pooled
    mixed_ref[...] = mixed_sum
    unit_ref[...] = unit
    inv_ref[...] = inv


def slope_kernel(
    after_ref, cut_ref, stem_ref, mix_ref, partner_ref,
    hidden_t_ref, patch_t_ref, stem_slope_ref, mix_slope_ref, mate_ref,
):
    del after_ref
    mate_ref[...] = partner_ref[...].astype(F32)
    nodes = cut_ref.shape[0]
    voxels = stem_ref.shape[0]
    width = 2 * voxels
    blocks = cut_ref.shape[1] // width
    stem2 = paired(stem_ref[...])
    mix2 = paired(mix_ref[...])
    for first in range(0, blocks, GROUP):
        number = min(GROUP, blocks - first)
        rows = slice(first * nodes, (first + number) * nodes)
        patches = pair_rows(cut_ref, width, first, number)
        pre_stem = nn(patches, stem2)
        sigma = sigmoid(pre_stem)
        scaled = pre_stem * sigma
        hidden = scaled.astype(BF16)
        stem_slope_ref[rows, :] = sigma + scaled * (1.0 - sigma)
        pre_mix = nn(hidden, mix2)
        sigma = sigmoid(pre_mix)
        mix_slope_ref[rows, :] = sigma + pre_mix * sigma * (1.0 - sigma)
        hidden_t_ref[:, rows] = hidden.T
        patch_t_ref[:, rows] = patches.T


def slot_tables(gathered_ref, embed_dim, max_nodes):
    slots = gathered_ref.shape[0]
    owners = slots // max_nodes
    lane = lax.broadcasted_iota(jnp.int32, (8, gathered_ref.shape[1]), 1)
    pick = jnp.where(lane == embed_dim, 1.0, 0.0).astype(BF16)
    count = nt(pick, gathered_ref[...])
    slot = lax.broadcasted_iota(jnp.int32, (8, slots), 1)
    heads = jnp.where(slot % max_nodes == 0, count, 0.0)
    step = min(slots, 512)
    row = lax.broadcasted_iota(jnp.int32, (step, slots), 0)
    column_owner = lax.broadcasted_iota(jnp.int32, (step, slots), 1) // max_nodes
    offset = jnp.zeros((8, slots), F32)
    for first in range(0, slots, step):
        earlier = jnp.where((row + first) // max_nodes < column_owner, 1.0, 0.0).astype(BF16)
        offset = offset + nn(heads[:, first : first + step].astype(BF16), earlier)
    del owners
    return count[0:1], offset[0:1], heads[0:1]


def score_sums(gathered_ref, embed_dim, max_nodes, live_row):
    slots = gathered_ref.shape[0]
    step = min(slots, 256)
    whole = gathered_ref[:, :embed_dim]

    def block(first, total):
        part = gathered_ref[pl.ds(first, step), :]
        scores = nt(part[:, :embed_dim], whole) / TEMPERATURE
        count = part[:, embed_dim : embed_dim + 1].astype(F32)
        row = lax.broadcasted_iota(jnp.int32, (step, 1), 0) + first
        live = (row % max_nodes).astype(F32) < count
        column = lax.broadcasted_iota(jnp.int32, scores.shape, 1)
        keep = jnp.logical_and(live, column != row)
        return total + jnp.sum(jnp.where(keep, jnp.exp(scores), 0.0), axis=0, keepdims=True)

    total = jnp.zeros((1, slots), F32)
    if slots == step:
        total = block(0, total)
    else:
        total = lax.fori_loop(
            0, slots // step, lambda i, t: block(pl.multiple_of(i * step, step), t), total
        )
    return jnp.where(live_row, total, 1.0)


def look_up(table_ref, number):
    shape = (number.shape[0], table_ref.shape[1])
    listed = lax.broadcasted_iota(jnp.int32, shape, 1).astype(F32)
    return jnp.sum(jnp.where(listed == number, table_ref[...], 0.0), axis=1, keepdims=True)


def backward_kernel(
    gathered_ref, mate_ref, pooled_ref, mixed_ref, unit_ref, inv_ref,
    hidden_t_ref, patch_t_ref, stem_slope_ref, mix_slope_ref, mix_ref, out_ref, proj_ref, grad_ref, loss_ref,
):
    nodes, embed_dim = unit_ref.shape
    slots = gathered_ref.shape[0]
    place = lax.axis_index("vol")
    channels = mix_ref.shape[0]
    voxels = patch_t_ref.shape[0] // 2
    blocks = stem_slope_ref.shape[0] // nodes

    count_row, offset_row, heads = slot_tables(gathered_ref, embed_dim, nodes)
    slot_row = lax.broadcasted_iota(jnp.int32, (1, slots), 1)
    within = (slot_row % nodes).astype(F32)
    live_row = within < count_row
    number_row = jnp.where(live_row, offset_row + within, -1.0)
    totals = score_sums(gathered_ref, embed_dim, nodes, live_row)

    own_offset = jnp.sum(
        jnp.where(slot_row // nodes < place, heads, 0.0), axis=1, keepdims=True
    )
    rank = lax.broadcasted_iota(jnp.int32, (nodes, 1), 0)
    own_number = own_offset + rank.astype(F32)
    mate = look_up(mate_ref, own_number)
    companion = jnp.where(number_row == mate, 1.0, 0.0).astype(BF16)

    whole = gathered_ref[:, :embed_dim]
    own = gathered_ref[pl.ds(pl.multiple_of(place * nodes, nodes), nodes), :]
    own_live = rank.astype(F32) < own[:, embed_dim : embed_dim + 1].astype(F32)
    scores = nt(own[:, :embed_dim], whole) / TEMPERATURE
    other = jnp.logical_and(live_row, slot_row != rank + place * nodes)
    weight = jnp.where(other, jnp.exp(scores), 0.0)
    own_total = jnp.sum(weight, axis=1, keepdims=True)
    row_weight = (weight * (1.0 / own_total)).astype(BF16)
    column_weight = (weight * (1.0 / totals)).astype(BF16)
    mixed_rows = nn(jnp.concatenate([row_weight, column_weight, companion], axis=0), whole)
    d_embed = (
        mixed_rows[:nodes] + mixed_rows[nodes : 2 * nodes] - 2.0 * mixed_rows[2 * nodes :]
    ) / TEMPERATURE

    node_dev = loss_ref.shape[1]
    owners = slots // nodes
    wanted = (lax.broadcasted_iota(jnp.int32, (node_dev, 1), 0) * owners + place).astype(F32)
    mine = number_row == wanted
    total = jnp.sum(jnp.where(mine, totals, 0.0), axis=1, keepdims=True)
    anchor = nn(jnp.where(mine, 1.0, 0.0).astype(BF16), whole)
    other_end = number_row == look_up(mate_ref, wanted)
    other_end = nn(jnp.where(other_end, 1.0, 0.0).astype(BF16), whole)
    loss = jnp.log(total) - jnp.sum(anchor * other_end, axis=1, keepdims=True) / TEMPERATURE
    row = lax.broadcasted_iota(jnp.int32, (node_dev, node_dev), 0)
    column = lax.broadcasted_iota(jnp.int32, (node_dev, node_dev), 1)
    loss_ref[...] = jnp.sum(jnp.where(row == column, loss, 0.0), axis=0, keepdims=True)

    unit = unit_ref[...]
    radial = jnp.sum(unit * d_embed, axis=1, keepdims=True)
    d_raw = jnp.where(own_live, inv_ref[...] * (d_embed - unit * radial), 0.0).astype(BF16)
    g_proj = tn(d_raw, pooled_ref[...])
    d_sum = (nn(d_raw, proj_ref[...]) / (2 * blocks)).astype(BF16)
    high, low = split(mixed_ref[...])
    g_out = tn(high, d_sum) + tn(low, d_sum)
    d_mixed = nt(d_sum, out_ref[...])
    d_mixed = jnp.concatenate([d_mixed, d_mixed], axis=1)
    d_pool = d_sum.astype(F32)
    d_pool = jnp.concatenate([d_pool, d_pool], axis=1)
    mix2 = paired(mix_ref[...])

    g_mix = jnp.zeros((2 * channels, 2 * channels), F32)
    g_stem = jnp.zeros((2 * voxels, 2 * channels), F32)
    chunk = 2 * GROUP
    for first in range(0, blocks, chunk):
        number = min(chunk, blocks - first)
        rows = slice(first * nodes, (first + number) * nodes)
        d_pre_mix = jnp.concatenate(
            [
                (d_mixed * mix_slope_ref[(first + i) * nodes : (first + i + 1) * nodes, :]).astype(BF16)
                for i in range(number)
            ],
            axis=0,
        )
        g_mix = g_mix + nn(hidden_t_ref[:, rows], d_pre_mix)
        back = nt(d_pre_mix, mix2)
        d_pre_stem = jnp.concatenate(
            [
                (
                    (d_pool + back[i * nodes : (i + 1) * nodes])
                    * stem_slope_ref[(first + i) * nodes : (first + i + 1) * nodes, :]
                ).astype(BF16)
                for i in range(number)
            ],
            axis=0,
        )
        g_stem = g_stem + nn(patch_t_ref[:, rows], d_pre_stem)
    g_mix = g_mix[:channels, :channels] + g_mix[channels:, channels:]
    g_stem = g_stem[:voxels, :channels] + g_stem[voxels:, channels:]
    grads = jnp.concatenate([g_stem, g_mix, g_out, g_proj], axis=0)
    grad_ref[...] = grads.reshape(grad_ref.shape).astype(grad_ref.dtype)


def share_kernel(part_ref, send_ref, *, devices):
    parts = part_ref[...].astype(F32)
    total = jnp.sum(parts.reshape((devices, -1) + parts.shape[1:]), axis=0, keepdims=True)
    total = jnp.broadcast_to(total.astype(send_ref.dtype), (devices,) + total.shape[1:])
    send_ref[...] = total.reshape(send_ref.shape)


def update_kernel(grad_ref, *refs):
    value = grad_ref[...].astype(F32).reshape(-1, grad_ref.shape[-1])
    start = 0
    for ref in refs:
        rows = ref.shape[0]
        grad = value[start : start + rows]
        start += rows
        squares = jnp.sum(jnp.sum(grad * grad, axis=0, keepdims=True), axis=1, keepdims=True)
        ref[...] = grad * lax.rsqrt(squares / (rows * ref.shape[1]) + RMS_EPS)


def vmem(number):
    return [pl.BlockSpec(memory_space=pltpu.VMEM)] * number


def anywhere(number):
    return [pl.BlockSpec(memory_space=pl.ANY)] * number


def hbm(number):
    return [pl.BlockSpec(memory_space=pltpu.HBM)] * number


def on_device(cutouts, counts, partner, w_stem, w_mix, w_out, w_proj):
    axes = ("vol", "rep")
    owners = lax.axis_size("vol")
    devices = owners * lax.axis_size("rep")
    cut = cutouts[0]
    nodes = cut.shape[0]
    voxels, channels = w_stem.shape
    embed_dim = w_proj.shape[1]
    rows = cut.shape[1] // (2 * voxels) * nodes
    groups = (cut.shape[1] // (2 * voxels) + GROUP - 1) // GROUP
    w_proj = w_proj.T
    weights = (w_stem, w_mix, w_out, w_proj)
    shape = jax.ShapeDtypeStruct
    params = pltpu.CompilerParams(vmem_limit_bytes=(16 << 20) + owners * nodes * 8192)

    send, pooled, mixed_sum, unit, inv = pl.pallas_call(
        forward_kernel,
        out_shape=(
            shape((owners, nodes, 2 * embed_dim), BF16),
            shape((nodes, channels), BF16),
            shape((nodes, channels), F32),
            shape((nodes, embed_dim), F32),
            shape((nodes, 1), F32),
        ),
        in_specs=[pl.BlockSpec(memory_space=pltpu.SMEM)] + hbm(5),
        out_specs=tuple(vmem(5)),
        scratch_shapes=[pltpu.VMEM(a.shape, BF16) for a in (cut,) + weights]
        + [pltpu.SemaphoreType.DMA((4,)), pltpu.SemaphoreType.DMA((groups,))],
        compiler_params=params,
        name="forward",
    )(counts, *(pltpu.with_memory_space_constraint(a, pltpu.HBM) for a in (cut, *weights)))

    gathered = lax.all_to_all(send, "vol", 0, 0).reshape(owners * nodes, 2 * embed_dim)

    hidden_t, patch_t, stem_slope, mix_slope, mates = pl.pallas_call(
        slope_kernel,
        out_shape=(
            shape((2 * channels, rows), BF16),
            shape((2 * voxels, rows), BF16),
            shape((rows, 2 * channels), F32),
            shape((rows, 2 * channels), F32),
            shape(partner.shape, F32),
        ),
        in_specs=anywhere(1) + vmem(4),
        out_specs=tuple(vmem(5)),
        compiler_params=params,
        name="slopes",
    )(pooled, cut, w_stem, w_mix, partner)

    total_rows = sum(w.shape[0] for w in weights)
    share = (total_rows + devices - 1) // devices
    tile = next(t for t in (8, 4, 2, 1) if share % t == 0)
    padded = share * devices - total_rows
    parts, loss = pl.pallas_call(
        backward_kernel,
        out_shape=(
            shape((total_rows, channels) if padded else (total_rows // tile, tile, channels), BF16),
            shape((1, partner.shape[1] // owners), F32),
        ),
        in_specs=vmem(13),
        out_specs=tuple(vmem(2)),
        compiler_params=params,
        name="backward",
    )(
        gathered, mates, pooled, mixed_sum, unit, inv,
        hidden_t, patch_t, stem_slope, mix_slope, w_mix, w_out, w_proj,
    )
    if padded:
        parts = jnp.pad(parts, ((0, padded), (0, 0))).reshape(-1, tile, channels)
    parts = lax.all_to_all(parts, axes, 0, 0, tiled=True)
    whole = pl.pallas_call(
        lambda *refs: share_kernel(*refs, devices=devices),
        out_shape=shape(parts.shape, BF16),
        in_specs=vmem(1),
        out_specs=vmem(1)[0],
        compiler_params=params,
        name="share",
    )(parts)
    whole = lax.all_to_all(whole, axes, 0, 0, tiled=True)
    if padded:
        whole = whole.reshape(-1, channels)[:total_rows]

    updates = pl.pallas_call(
        update_kernel,
        out_shape=tuple(shape(w.shape, F32) for w in weights),
        in_specs=vmem(1),
        out_specs=tuple(vmem(4)),
        compiler_params=params,
        name="updates",
    )(whole)
    return (*updates[:3], updates[3].T, loss[None])


def solution(mesh):
    in_specs = (P("rep", "vol", None), P("rep", "vol"), P("rep", None), P(), P(), P(), P())
    out_specs = (P(), P(), P(), P(), P("rep", "vol", None))
    return jax.shard_map(
        on_device, mesh=mesh, in_specs=in_specs, out_specs=out_specs, check_vma=False
    )
```

```python
import jax
import jax.numpy as jnp
from jax import lax
from jax.experimental import pallas as pl
from jax.experimental.pallas import tpu as pltpu
from jax.sharding import PartitionSpec as P

TEMPERATURE = 0.2
NORM_EPS = 1e-06
RMS_EPS = 1e-06
BF16 = jnp.bfloat16
F32 = jnp.float32
GROUP = 16


def nn(left, right):
    return lax.dot_general(left, right, (((1,), (0,)), ((), ())), preferred_element_type=F32)


def nt(left, right):
    return lax.dot_general(left, right, (((1,), (1,)), ((), ())), preferred_element_type=F32)


def tn(left, right):
    return lax.dot_general(left, right, (((0,), (0,)), ((), ())), preferred_element_type=F32)


def split(value):
    high = value.astype(BF16)
    low = (value - high.astype(F32)).astype(BF16)
    return high, low


def paired(weight):
    zero = jnp.zeros_like(weight)
    return jnp.concatenate(
        [
            jnp.concatenate([weight, zero], axis=1),
            jnp.concatenate([zero, weight], axis=1),
        ],
        axis=0,
    )


def pair_rows(cut_ref, width, first, number):
    return jnp.concatenate(
        [cut_ref[:, (first + i) * width : (first + i + 1) * width] for i in range(number)], axis=0
    )


def forward_kernel(
    count_ref, cut_hbm, stem_hbm, mix_hbm, out_hbm, proj_hbm, partner_hbm,
    send_ref, pooled_ref, mixed_ref, unit_ref, inv_ref, hidden_t_ref, patch_t_ref,
    stem_slope_ref, mix_slope_ref, mate_ref, half_mix_ref, out_ref, proj_ref,
    cut_ref, stem_ref, mix_ref, partner_ref, sems,
):
    nodes = cut_ref.shape[0]
    voxels, channels = stem_ref.shape
    width = 2 * voxels
    blocks = cut_ref.shape[1] // width
    pairs = (
        (cut_hbm, cut_ref), (stem_hbm, stem_ref), (mix_hbm, mix_ref),
        (out_hbm, out_ref), (proj_hbm, proj_ref), (partner_hbm, partner_ref),
    )
    copies = [
        pltpu.make_async_copy(source, target, sems.at[i])
        for i, (source, target) in enumerate(pairs)
    ]
    for each in copies:
        each.start()
    for each in copies:
        each.wait()
    mate_ref[...] = partner_ref[...].astype(F32)
    stem2 = paired((stem_ref[...].astype(F32) * 0.5).astype(BF16))
    mix2 = paired((mix_ref[...].astype(F32) * 0.5).astype(BF16))
    half_mix_ref[...] = mix2
    hidden_sum = jnp.zeros((nodes, 2 * channels), F32)
    mixed_sum = jnp.zeros((nodes, 2 * channels), F32)
    for first in range(0, blocks, GROUP):
        number = min(GROUP, blocks - first)
        rows = slice(first * nodes, (first + number) * nodes)
        patches = pair_rows(cut_ref, width, first, number)
        half = nn(patches, stem2)
        t = jnp.tanh(half)
        hidden = half + half * t
        stem_slope_ref[rows, :] = (1.0 + t) + (hidden - hidden * t)
        narrow = hidden.astype(BF16)
        half = nn(narrow, mix2)
        t = jnp.tanh(half)
        mixed = half + half * t
        mix_slope_ref[rows, :] = (1.0 + t) + (mixed - mixed * t)
        for i in range(number):
            part = slice(i * nodes, (i + 1) * nodes)
            hidden_sum = hidden_sum + hidden[part]
            mixed_sum = mixed_sum + mixed[part]
        hidden_t_ref[:, rows] = narrow.T
        patch_t_ref[:, rows] = patches.T
    hidden_sum = hidden_sum[:, :channels] + hidden_sum[:, channels:]
    mixed_sum = mixed_sum[:, :channels] + mixed_sum[:, channels:]
    high, low = split(mixed_sum)
    weight = out_ref[...]
    summed = hidden_sum + (nn(high, weight) + nn(low, weight))
    pooled = (summed / (2 * blocks)).astype(BF16)
    raw = nt(pooled, proj_ref[...])
    inv = lax.rsqrt(jnp.sum(raw * raw, axis=1, keepdims=True) + NORM_EPS)
    unit = raw * inv
    count = count_ref[0, 0]
    live = lax.broadcasted_iota(jnp.int32, unit.shape, 0) < count
    embed = jnp.where(live, unit, 0.0)
    counts = jnp.zeros(unit.shape, F32) + count.astype(F32)
    send = jnp.concatenate([embed, counts], axis=1).astype(BF16)
    send_ref[...] = jnp.broadcast_to(send[None], send_ref.shape)
    pooled_ref[...] = pooled
    mixed_ref[...] = mixed_sum
    unit_ref[...] = unit
    inv_ref[...] = inv


def slot_tables(gathered_ref, embed_dim, max_nodes):
    slots = gathered_ref.shape[0]
    owners = slots // max_nodes
    lane = lax.broadcasted_iota(jnp.int32, (8, gathered_ref.shape[1]), 1)
    pick = jnp.where(lane == embed_dim, 1.0, 0.0).astype(BF16)
    count = nt(pick, gathered_ref[...])
    slot = lax.broadcasted_iota(jnp.int32, (8, slots), 1)
    heads = jnp.where(slot % max_nodes == 0, count, 0.0)
    step = min(slots, 512)
    row = lax.broadcasted_iota(jnp.int32, (step, slots), 0)
    column_owner = lax.broadcasted_iota(jnp.int32, (step, slots), 1) // max_nodes
    offset = jnp.zeros((8, slots), F32)
    for first in range(0, slots, step):
        earlier = jnp.where((row + first) // max_nodes < column_owner, 1.0, 0.0).astype(BF16)
        offset = offset + nn(heads[:, first : first + step].astype(BF16), earlier)
    del owners
    return count[0:1], offset[0:1], heads[0:1]


def score_sums(gathered_ref, embed_dim, max_nodes, live_row):
    slots = gathered_ref.shape[0]
    step = min(slots, 256)
    whole = gathered_ref[:, :embed_dim]

    def block(first, total):
        part = gathered_ref[pl.ds(first, step), :]
        scores = nt(part[:, :embed_dim], whole) / TEMPERATURE
        count = part[:, embed_dim : embed_dim + 1].astype(F32)
        row = lax.broadcasted_iota(jnp.int32, (step, 1), 0) + first
        live = (row % max_nodes).astype(F32) < count
        column = lax.broadcasted_iota(jnp.int32, scores.shape, 1)
        keep = jnp.logical_and(live, column != row)
        return total + jnp.sum(jnp.where(keep, jnp.exp(scores), 0.0), axis=0, keepdims=True)

    total = jnp.zeros((1, slots), F32)
    if slots == step:
        total = block(0, total)
    else:
        total = lax.fori_loop(
            0, slots // step, lambda i, t: block(pl.multiple_of(i * step, step), t), total
        )
    return jnp.where(live_row, total, 1.0)


def look_up(table_ref, number):
    shape = (number.shape[0], table_ref.shape[1])
    listed = lax.broadcasted_iota(jnp.int32, shape, 1).astype(F32)
    return jnp.sum(jnp.where(listed == number, table_ref[...], 0.0), axis=1, keepdims=True)


def backward_kernel(
    gathered_ref, mate_ref, pooled_ref, mixed_ref, unit_ref, inv_ref,
    hidden_t_ref, patch_t_ref, stem_slope_ref, mix_slope_ref, half_mix_ref, out_ref, proj_ref,
    grad_ref, loss_ref,
):
    nodes, embed_dim = unit_ref.shape
    slots = gathered_ref.shape[0]
    place = lax.axis_index("vol")
    channels = out_ref.shape[0]
    voxels = patch_t_ref.shape[0] // 2
    blocks = stem_slope_ref.shape[0] // nodes

    count_row, offset_row, heads = slot_tables(gathered_ref, embed_dim, nodes)
    slot_row = lax.broadcasted_iota(jnp.int32, (1, slots), 1)
    within = (slot_row % nodes).astype(F32)
    live_row = within < count_row
    number_row = jnp.where(live_row, offset_row + within, -1.0)
    totals = score_sums(gathered_ref, embed_dim, nodes, live_row)

    own_offset = jnp.sum(
        jnp.where(slot_row // nodes < place, heads, 0.0), axis=1, keepdims=True
    )
    rank = lax.broadcasted_iota(jnp.int32, (nodes, 1), 0)
    own_number = own_offset + rank.astype(F32)
    mate = look_up(mate_ref, own_number)
    companion = jnp.where(number_row == mate, 1.0, 0.0).astype(BF16)

    whole = gathered_ref[:, :embed_dim]
    own = gathered_ref[pl.ds(pl.multiple_of(place * nodes, nodes), nodes), :]
    own_live = rank.astype(F32) < own[:, embed_dim : embed_dim + 1].astype(F32)
    scores = nt(own[:, :embed_dim], whole) / TEMPERATURE
    other = jnp.logical_and(live_row, slot_row != rank + place * nodes)
    weight = jnp.where(other, jnp.exp(scores), 0.0)
    own_total = jnp.sum(weight, axis=1, keepdims=True)
    row_weight = (weight * (1.0 / own_total)).astype(BF16)
    column_weight = (weight * (1.0 / totals)).astype(BF16)
    mixed_rows = nn(jnp.concatenate([row_weight, column_weight, companion], axis=0), whole)
    d_embed = (
        mixed_rows[:nodes] + mixed_rows[nodes : 2 * nodes] - 2.0 * mixed_rows[2 * nodes :]
    ) / TEMPERATURE

    node_dev = loss_ref.shape[1]
    owners = slots // nodes
    wanted = (lax.broadcasted_iota(jnp.int32, (node_dev, 1), 0) * owners + place).astype(F32)
    mine = number_row == wanted
    total = jnp.sum(jnp.where(mine, totals, 0.0), axis=1, keepdims=True)
    anchor = nn(jnp.where(mine, 1.0, 0.0).astype(BF16), whole)
    other_end = number_row == look_up(mate_ref, wanted)
    other_end = nn(jnp.where(other_end, 1.0, 0.0).astype(BF16), whole)
    loss = jnp.log(total) - jnp.sum(anchor * other_end, axis=1, keepdims=True) / TEMPERATURE
    row = lax.broadcasted_iota(jnp.int32, (node_dev, node_dev), 0)
    column = lax.broadcasted_iota(jnp.int32, (node_dev, node_dev), 1)
    loss_ref[...] = jnp.sum(jnp.where(row == column, loss, 0.0), axis=0, keepdims=True)

    unit = unit_ref[...]
    radial = jnp.sum(unit * d_embed, axis=1, keepdims=True)
    d_raw = jnp.where(own_live, inv_ref[...] * (d_embed - unit * radial), 0.0).astype(BF16)
    g_proj = tn(d_raw, pooled_ref[...])
    d_sum = (nn(d_raw, proj_ref[...]) / (2 * blocks)).astype(BF16)
    high, low = split(mixed_ref[...])
    g_out = tn(high, d_sum) + tn(low, d_sum)
    d_mixed = 0.5 * nt(d_sum, out_ref[...])
    d_mixed = jnp.concatenate([d_mixed, d_mixed], axis=1)
    d_pool = 0.5 * d_sum.astype(F32)
    d_pool = jnp.concatenate([d_pool, d_pool], axis=1)
    half_mix = half_mix_ref[...]

    g_mix = jnp.zeros((2 * channels, 2 * channels), F32)
    g_stem = jnp.zeros((2 * voxels, 2 * channels), F32)
    chunk = 2 * GROUP
    for first in range(0, blocks, chunk):
        number = min(chunk, blocks - first)
        rows = slice(first * nodes, (first + number) * nodes)
        d_pre_mix = jnp.concatenate(
            [
                (d_mixed * mix_slope_ref[(first + i) * nodes : (first + i + 1) * nodes, :]).astype(BF16)
                for i in range(number)
            ],
            axis=0,
        )
        g_mix = g_mix + nn(hidden_t_ref[:, rows], d_pre_mix)
        back = nt(d_pre_mix, half_mix)
        d_pre_stem = jnp.concatenate(
            [
                (
                    (d_pool + back[i * nodes : (i + 1) * nodes])
                    * stem_slope_ref[(first + i) * nodes : (first + i + 1) * nodes, :]
                ).astype(BF16)
                for i in range(number)
            ],
            axis=0,
        )
        g_stem = g_stem + nn(patch_t_ref[:, rows], d_pre_stem)
    g_mix = g_mix[:channels, :channels] + g_mix[channels:, channels:]
    g_stem = g_stem[:voxels, :channels] + g_stem[voxels:, channels:]
    grads = jnp.concatenate([g_stem, g_mix, g_out, g_proj], axis=0)
    grad_ref[...] = grads.reshape(grad_ref.shape).astype(grad_ref.dtype)


def share_kernel(part_ref, send_ref, *, devices):
    parts = part_ref[...].astype(F32)
    total = jnp.sum(parts.reshape((devices, -1) + parts.shape[1:]), axis=0, keepdims=True)
    total = jnp.broadcast_to(total.astype(send_ref.dtype), (devices,) + total.shape[1:])
    send_ref[...] = total.reshape(send_ref.shape)


def update_kernel(grad_ref, own_loss_ref, *refs):
    *refs, loss_ref = refs
    loss_ref[...] = own_loss_ref[...]
    value = grad_ref[...].astype(F32).reshape(-1, grad_ref.shape[-1])
    start = 0
    for ref in refs:
        rows = ref.shape[0]
        grad = value[start : start + rows]
        start += rows
        squares = jnp.sum(jnp.sum(grad * grad, axis=0, keepdims=True), axis=1, keepdims=True)
        ref[...] = grad * lax.rsqrt(squares / (rows * ref.shape[1]) + RMS_EPS)


def vmem(number):
    return [pl.BlockSpec(memory_space=pltpu.VMEM)] * number


def hbm(number):
    return [pl.BlockSpec(memory_space=pltpu.HBM)] * number


def on_device(cutouts, counts, partner, w_stem, w_mix, w_out, w_proj):
    axes = ("vol", "rep")
    owners = lax.axis_size("vol")
    devices = owners * lax.axis_size("rep")
    cut = cutouts[0]
    nodes = cut.shape[0]
    voxels, channels = w_stem.shape
    embed_dim = w_proj.shape[1]
    rows = cut.shape[1] // (2 * voxels) * nodes
    w_proj = w_proj.T
    weights = (w_stem, w_mix, w_out, w_proj)
    shape = jax.ShapeDtypeStruct
    params = pltpu.CompilerParams(vmem_limit_bytes=(16 << 20) + owners * nodes * 8192)

    pin = pltpu.with_memory_space_constraint
    send, *saved = pl.pallas_call(
        forward_kernel,
        out_shape=(
            shape((owners, nodes, 2 * embed_dim), BF16),
            shape((nodes, channels), BF16),
            shape((nodes, channels), F32),
            shape((nodes, embed_dim), F32),
            shape((nodes, 1), F32),
            shape((2 * channels, rows), BF16),
            shape((2 * voxels, rows), BF16),
            shape((rows, 2 * channels), F32),
            shape((rows, 2 * channels), F32),
            shape(partner.shape, F32),
            shape((2 * channels, 2 * channels), BF16),
            shape(w_out.shape, BF16),
            shape(w_proj.shape, BF16),
        ),
        in_specs=[pl.BlockSpec(memory_space=pltpu.SMEM)] + hbm(6),
        out_specs=tuple(vmem(13)),
        scratch_shapes=[
            pltpu.VMEM(cut.shape, BF16),
            pltpu.VMEM(w_stem.shape, BF16),
            pltpu.VMEM(w_mix.shape, BF16),
            pltpu.VMEM(partner.shape, jnp.int32),
            pltpu.SemaphoreType.DMA((6,)),
        ],
        compiler_params=params,
        name="forward",
    )(counts, *(pin(a, pltpu.HBM) for a in (cut, *weights, partner)))
    pooled, mixed_sum, unit, inv, hidden_t, patch_t, stem_slope, mix_slope, mates, *rest = saved

    gathered = lax.all_to_all(send, "vol", 0, 0).reshape(owners * nodes, 2 * embed_dim)

    total_rows = sum(w.shape[0] for w in weights)
    share = (total_rows + devices - 1) // devices
    tile = next(t for t in (8, 4, 2, 1) if share % t == 0)
    padded = share * devices - total_rows
    parts, loss = pl.pallas_call(
        backward_kernel,
        out_shape=(
            shape((total_rows, channels) if padded else (total_rows // tile, tile, channels), BF16),
            shape((1, partner.shape[1] // owners), F32),
        ),
        in_specs=vmem(13),
        out_specs=tuple(vmem(2)),
        compiler_params=params,
        name="backward",
    )(
        gathered, mates, pooled, mixed_sum, unit, inv,
        hidden_t, patch_t, stem_slope, mix_slope, *rest,
    )
    if padded:
        parts = jnp.pad(parts, ((0, padded), (0, 0))).reshape(-1, tile, channels)
    parts = lax.all_to_all(parts, axes, 0, 0, tiled=True)
    whole = pl.pallas_call(
        lambda *refs: share_kernel(*refs, devices=devices),
        out_shape=shape(parts.shape, BF16),
        in_specs=vmem(1),
        out_specs=vmem(1)[0],
        compiler_params=params,
        name="share",
    )(parts)
    whole = lax.all_to_all(whole, axes, 0, 0, tiled=True)
    if padded:
        whole = whole.reshape(-1, channels)[:total_rows]

    updates = pl.pallas_call(
        update_kernel,
        out_shape=tuple(shape(w.shape, F32) for w in weights) + (shape(loss.shape, F32),),
        in_specs=vmem(2),
        out_specs=tuple(vmem(5)),
        compiler_params=params,
        name="updates",
    )(whole, loss)
    return (*updates[:3], updates[3].T, updates[4][None])


def solution(mesh):
    in_specs = (P("rep", "vol", None), P("rep", "vol"), P("rep", None), P(), P(), P(), P())
    out_specs = (P(), P(), P(), P(), P("rep", "vol", None))
    return jax.shard_map(
        on_device, mesh=mesh, in_specs=in_specs, out_specs=out_specs, check_vma=False
    )
```

```python
import jax
import jax.numpy as jnp
from jax import lax
from jax.experimental import pallas as pl
from jax.experimental.pallas import tpu as pltpu
from jax.sharding import PartitionSpec as P

TEMPERATURE = 0.2
NORM_EPS = 1e-06
RMS_EPS = 1e-06
BF16 = jnp.bfloat16
F32 = jnp.float32
GROUP = 16


def nn(left, right):
    return lax.dot_general(left, right, (((1,), (0,)), ((), ())), preferred_element_type=F32)


def nt(left, right):
    return lax.dot_general(left, right, (((1,), (1,)), ((), ())), preferred_element_type=F32)


def tn(left, right):
    return lax.dot_general(left, right, (((0,), (0,)), ((), ())), preferred_element_type=F32)


def split(value):
    high = value.astype(BF16)
    low = (value - high.astype(F32)).astype(BF16)
    return high, low


def paired(weight):
    zero = jnp.zeros_like(weight)
    return jnp.concatenate(
        [
            jnp.concatenate([weight, zero], axis=1),
            jnp.concatenate([zero, weight], axis=1),
        ],
        axis=0,
    )


def pair_rows(cut_ref, width, first, number):
    return jnp.concatenate(
        [cut_ref[:, (first + i) * width : (first + i + 1) * width] for i in range(number)], axis=0
    )


def first_kernel(first_ref):
    first_ref[...] = jnp.zeros(first_ref.shape, first_ref.dtype)


def forward_kernel(
    first_ref, count_ref, cut_ref, stem_ref, mix_ref, out_in, proj_in, partner_hbm,
    send_ref, pooled_ref, mixed_ref, unit_ref, inv_ref, hidden_t_ref, patch_t_ref,
    stem_slope_ref, mix_slope_ref, mate_ref, half_mix_ref, out_ref, proj_ref,
    partner_ref, sem,
):
    nodes = cut_ref.shape[0]
    voxels, channels = stem_ref.shape
    width = 2 * voxels
    blocks = cut_ref.shape[1] // width
    del first_ref
    out_ref[...] = out_in[...]
    proj_ref[...] = proj_in[...]
    partner_copy = pltpu.make_async_copy(partner_hbm, partner_ref, sem)
    partner_copy.start()
    stem2 = paired((stem_ref[...].astype(F32) * 0.5).astype(BF16))
    mix2 = paired((mix_ref[...].astype(F32) * 0.5).astype(BF16))
    half_mix_ref[...] = mix2
    hidden_sum = jnp.zeros((nodes, 2 * channels), F32)
    mixed_sum = jnp.zeros((nodes, 2 * channels), F32)
    for first in range(0, blocks, GROUP):
        number = min(GROUP, blocks - first)
        rows = slice(first * nodes, (first + number) * nodes)
        patches = pair_rows(cut_ref, width, first, number)
        half = nn(patches, stem2)
        t = jnp.tanh(half)
        u = 1.0 + t
        hidden = half * u
        stem_slope_ref[rows, :] = u + hidden * (1.0 - t)
        narrow = hidden.astype(BF16)
        half = nn(narrow, mix2)
        t = jnp.tanh(half)
        u = 1.0 + t
        mixed = half * u
        mix_slope_ref[rows, :] = u + mixed * (1.0 - t)
        for i in range(number):
            part = slice(i * nodes, (i + 1) * nodes)
            hidden_sum = hidden_sum + hidden[part]
            mixed_sum = mixed_sum + mixed[part]
        hidden_t_ref[:, rows] = narrow.T
        patch_t_ref[:, rows] = patches.T
    hidden_sum = hidden_sum[:, :channels] + hidden_sum[:, channels:]
    mixed_sum = mixed_sum[:, :channels] + mixed_sum[:, channels:]
    high, low = split(mixed_sum)
    weight = out_ref[...]
    summed = hidden_sum + (nn(high, weight) + nn(low, weight))
    pooled = (summed / (2 * blocks)).astype(BF16)
    raw = nt(pooled, proj_ref[...])
    inv = lax.rsqrt(jnp.sum(raw * raw, axis=1, keepdims=True) + NORM_EPS)
    unit = raw * inv
    count = count_ref[0, 0]
    live = lax.broadcasted_iota(jnp.int32, unit.shape, 0) < count
    embed = jnp.where(live, unit, 0.0)
    counts = jnp.zeros(unit.shape, F32) + count.astype(F32)
    send = jnp.concatenate([embed, counts], axis=1).astype(BF16)
    send_ref[...] = jnp.broadcast_to(send[None], send_ref.shape)
    partner_copy.wait()
    mate_ref[...] = partner_ref[...].astype(F32)
    pooled_ref[...] = pooled
    mixed_ref[...] = mixed_sum
    unit_ref[...] = unit
    inv_ref[...] = inv


def slot_tables(gathered_ref, embed_dim, max_nodes):
    slots = gathered_ref.shape[0]
    owners = slots // max_nodes
    lane = lax.broadcasted_iota(jnp.int32, (8, gathered_ref.shape[1]), 1)
    pick = jnp.where(lane == embed_dim, 1.0, 0.0).astype(BF16)
    count = nt(pick, gathered_ref[...])
    slot = lax.broadcasted_iota(jnp.int32, (8, slots), 1)
    heads = jnp.where(slot % max_nodes == 0, count, 0.0)
    step = min(slots, 512)
    row = lax.broadcasted_iota(jnp.int32, (step, slots), 0)
    column_owner = lax.broadcasted_iota(jnp.int32, (step, slots), 1) // max_nodes
    offset = jnp.zeros((8, slots), F32)
    for first in range(0, slots, step):
        earlier = jnp.where((row + first) // max_nodes < column_owner, 1.0, 0.0).astype(BF16)
        offset = offset + nn(heads[:, first : first + step].astype(BF16), earlier)
    del owners
    return count[0:1], offset[0:1], heads[0:1]


def score_sums(gathered_ref, embed_dim, max_nodes, live_row):
    slots = gathered_ref.shape[0]
    step = min(slots, 256)
    whole = gathered_ref[:, :embed_dim]

    def block(first, total):
        part = gathered_ref[pl.ds(first, step), :]
        scores = nt(part[:, :embed_dim], whole) / TEMPERATURE
        count = part[:, embed_dim : embed_dim + 1].astype(F32)
        row = lax.broadcasted_iota(jnp.int32, (step, 1), 0) + first
        live = (row % max_nodes).astype(F32) < count
        column = lax.broadcasted_iota(jnp.int32, scores.shape, 1)
        keep = jnp.logical_and(live, column != row)
        return total + jnp.sum(jnp.where(keep, jnp.exp(scores), 0.0), axis=0, keepdims=True)

    total = jnp.zeros((1, slots), F32)
    if slots == step:
        total = block(0, total)
    else:
        total = lax.fori_loop(
            0, slots // step, lambda i, t: block(pl.multiple_of(i * step, step), t), total
        )
    return jnp.where(live_row, total, 1.0)


def look_up(table_ref, number):
    shape = (number.shape[0], table_ref.shape[1])
    listed = lax.broadcasted_iota(jnp.int32, shape, 1).astype(F32)
    return jnp.sum(jnp.where(listed == number, table_ref[...], 0.0), axis=1, keepdims=True)


def backward_kernel(
    gathered_ref, mate_ref, pooled_ref, mixed_ref, unit_ref, inv_ref,
    hidden_t_ref, patch_t_ref, stem_slope_ref, mix_slope_ref, half_mix_ref, out_ref, proj_ref,
    grad_ref, loss_ref,
):
    nodes, embed_dim = unit_ref.shape
    slots = gathered_ref.shape[0]
    place = lax.axis_index("vol")
    channels = out_ref.shape[0]
    voxels = patch_t_ref.shape[0] // 2
    blocks = stem_slope_ref.shape[0] // nodes

    count_row, offset_row, heads = slot_tables(gathered_ref, embed_dim, nodes)
    slot_row = lax.broadcasted_iota(jnp.int32, (1, slots), 1)
    within = (slot_row % nodes).astype(F32)
    live_row = within < count_row
    number_row = jnp.where(live_row, offset_row + within, -1.0)
    totals = score_sums(gathered_ref, embed_dim, nodes, live_row)

    own_offset = jnp.sum(
        jnp.where(slot_row // nodes < place, heads, 0.0), axis=1, keepdims=True
    )
    rank = lax.broadcasted_iota(jnp.int32, (nodes, 1), 0)
    own_number = own_offset + rank.astype(F32)
    mate = look_up(mate_ref, own_number)
    companion = jnp.where(number_row == mate, 1.0, 0.0).astype(BF16)

    whole = gathered_ref[:, :embed_dim]
    own = gathered_ref[pl.ds(pl.multiple_of(place * nodes, nodes), nodes), :]
    own_live = rank.astype(F32) < own[:, embed_dim : embed_dim + 1].astype(F32)
    scores = nt(own[:, :embed_dim], whole) / TEMPERATURE
    other = jnp.logical_and(live_row, slot_row != rank + place * nodes)
    weight = jnp.where(other, jnp.exp(scores), 0.0)
    own_total = jnp.sum(weight, axis=1, keepdims=True)
    row_weight = (weight * (1.0 / own_total)).astype(BF16)
    column_weight = (weight * (1.0 / totals)).astype(BF16)
    mixed_rows = nn(jnp.concatenate([row_weight, column_weight, companion], axis=0), whole)
    d_embed = (
        mixed_rows[:nodes] + mixed_rows[nodes : 2 * nodes] - 2.0 * mixed_rows[2 * nodes :]
    ) / TEMPERATURE

    node_dev = loss_ref.shape[1]
    owners = slots // nodes
    wanted = (lax.broadcasted_iota(jnp.int32, (node_dev, 1), 0) * owners + place).astype(F32)
    mine = number_row == wanted
    total = jnp.sum(jnp.where(mine, totals, 0.0), axis=1, keepdims=True)
    anchor = nn(jnp.where(mine, 1.0, 0.0).astype(BF16), whole)
    other_end = number_row == look_up(mate_ref, wanted)
    other_end = nn(jnp.where(other_end, 1.0, 0.0).astype(BF16), whole)
    loss = jnp.log(total) - jnp.sum(anchor * other_end, axis=1, keepdims=True) / TEMPERATURE
    row = lax.broadcasted_iota(jnp.int32, (node_dev, node_dev), 0)
    column = lax.broadcasted_iota(jnp.int32, (node_dev, node_dev), 1)
    loss_ref[...] = jnp.sum(jnp.where(row == column, loss, 0.0), axis=0, keepdims=True)

    unit = unit_ref[...]
    radial = jnp.sum(unit * d_embed, axis=1, keepdims=True)
    d_raw = jnp.where(own_live, inv_ref[...] * (d_embed - unit * radial), 0.0).astype(BF16)
    g_proj = tn(d_raw, pooled_ref[...])
    d_sum = (nn(d_raw, proj_ref[...]) / (2 * blocks)).astype(BF16)
    high, low = split(mixed_ref[...])
    g_out = tn(high, d_sum) + tn(low, d_sum)
    d_mixed = 0.5 * nt(d_sum, out_ref[...])
    d_mixed = jnp.concatenate([d_mixed, d_mixed], axis=1)
    d_pool = 0.5 * d_sum.astype(F32)
    d_pool = jnp.concatenate([d_pool, d_pool], axis=1)
    half_mix = half_mix_ref[...]

    g_mix = jnp.zeros((2 * channels, 2 * channels), F32)
    g_stem = jnp.zeros((2 * voxels, 2 * channels), F32)
    chunk = 2 * GROUP
    for first in range(0, blocks, chunk):
        number = min(chunk, blocks - first)
        rows = slice(first * nodes, (first + number) * nodes)
        d_pre_mix = jnp.concatenate(
            [
                (d_mixed * mix_slope_ref[(first + i) * nodes : (first + i + 1) * nodes, :]).astype(BF16)
                for i in range(number)
            ],
            axis=0,
        )
        g_mix = g_mix + nn(hidden_t_ref[:, rows], d_pre_mix)
        back = nt(d_pre_mix, half_mix)
        d_pre_stem = jnp.concatenate(
            [
                (
                    (d_pool + back[i * nodes : (i + 1) * nodes])
                    * stem_slope_ref[(first + i) * nodes : (first + i + 1) * nodes, :]
                ).astype(BF16)
                for i in range(number)
            ],
            axis=0,
        )
        g_stem = g_stem + nn(patch_t_ref[:, rows], d_pre_stem)
    g_mix = g_mix[:channels, :channels] + g_mix[channels:, channels:]
    g_stem = g_stem[:voxels, :channels] + g_stem[voxels:, channels:]
    grads = jnp.concatenate([g_stem, g_mix, g_out, g_proj], axis=0)
    grad_ref[...] = grads.reshape(grad_ref.shape).astype(grad_ref.dtype)


def share_kernel(part_ref, send_ref, *, devices):
    parts = part_ref[...].astype(F32)
    total = jnp.sum(parts.reshape((devices, -1) + parts.shape[1:]), axis=0, keepdims=True)
    total = jnp.broadcast_to(total.astype(send_ref.dtype), (devices,) + total.shape[1:])
    send_ref[...] = total.reshape(send_ref.shape)


def update_kernel(grad_ref, own_loss_ref, *refs):
    *refs, loss_ref = refs
    loss_ref[...] = own_loss_ref[...]
    value = grad_ref[...].astype(F32).reshape(-1, grad_ref.shape[-1])
    start = 0
    for ref in refs:
        rows = ref.shape[0]
        grad = value[start : start + rows]
        start += rows
        squares = jnp.sum(jnp.sum(grad * grad, axis=0, keepdims=True), axis=1, keepdims=True)
        ref[...] = grad * lax.rsqrt(squares / (rows * ref.shape[1]) + RMS_EPS)


def vmem(number):
    return [pl.BlockSpec(memory_space=pltpu.VMEM)] * number


def hbm(number):
    return [pl.BlockSpec(memory_space=pltpu.HBM)] * number


def on_device(cutouts, counts, partner, w_stem, w_mix, w_out, w_proj):
    axes = ("vol", "rep")
    owners = lax.axis_size("vol")
    devices = owners * lax.axis_size("rep")
    cut = cutouts[0]
    nodes = cut.shape[0]
    voxels, channels = w_stem.shape
    embed_dim = w_proj.shape[1]
    rows = cut.shape[1] // (2 * voxels) * nodes
    w_proj = w_proj.T
    weights = (w_stem, w_mix, w_out, w_proj)
    shape = jax.ShapeDtypeStruct
    params = pltpu.CompilerParams(vmem_limit_bytes=(16 << 20) + owners * nodes * 8192)

    first = pl.pallas_call(
        first_kernel,
        out_shape=shape((8, 128), F32),
        out_specs=vmem(1)[0],
        compiler_params=params,
        cost_estimate=pl.CostEstimate(flops=10**9, transcendentals=10**6, bytes_accessed=10**8),
        name="first",
    )()
    send, *saved = pl.pallas_call(
        forward_kernel,
        out_shape=(
            shape((owners, nodes, 2 * embed_dim), BF16),
            shape((nodes, channels), BF16),
            shape((nodes, channels), F32),
            shape((nodes, embed_dim), F32),
            shape((nodes, 1), F32),
            shape((2 * channels, rows), BF16),
            shape((2 * voxels, rows), BF16),
            shape((rows, 2 * channels), F32),
            shape((rows, 2 * channels), F32),
            shape(partner.shape, F32),
            shape((2 * channels, 2 * channels), BF16),
            shape(w_out.shape, BF16),
            shape(w_proj.shape, BF16),
        ),
        in_specs=vmem(1) + [pl.BlockSpec(memory_space=pltpu.SMEM)] + vmem(5) + hbm(1),
        out_specs=tuple(vmem(13)),
        scratch_shapes=[pltpu.VMEM(partner.shape, jnp.int32), pltpu.SemaphoreType.DMA(())],
        compiler_params=params,
        name="forward",
    )(first, counts, cut, *weights, pltpu.with_memory_space_constraint(partner, pltpu.HBM))
    pooled, mixed_sum, unit, inv, hidden_t, patch_t, stem_slope, mix_slope, mates, *rest = saved

    gathered = lax.all_to_all(send, "vol", 0, 0).reshape(owners * nodes, 2 * embed_dim)

    total_rows = sum(w.shape[0] for w in weights)
    share = (total_rows + devices - 1) // devices
    tile = next(t for t in (8, 4, 2, 1) if share % t == 0)
    padded = share * devices - total_rows
    parts, loss = pl.pallas_call(
        backward_kernel,
        out_shape=(
            shape((total_rows, channels) if padded else (total_rows // tile, tile, channels), BF16),
            shape((1, partner.shape[1] // owners), F32),
        ),
        in_specs=vmem(13),
        out_specs=tuple(vmem(2)),
        compiler_params=params,
        name="backward",
    )(
        gathered, mates, pooled, mixed_sum, unit, inv,
        hidden_t, patch_t, stem_slope, mix_slope, *rest,
    )
    if padded:
        parts = jnp.pad(parts, ((0, padded), (0, 0))).reshape(-1, tile, channels)
    parts = lax.all_to_all(parts, axes, 0, 0, tiled=True)
    whole = pl.pallas_call(
        lambda *refs: share_kernel(*refs, devices=devices),
        out_shape=shape(parts.shape, BF16),
        in_specs=vmem(1),
        out_specs=vmem(1)[0],
        compiler_params=params,
        name="share",
    )(parts)
    whole = lax.all_to_all(whole, axes, 0, 0, tiled=True)
    if padded:
        whole = whole.reshape(-1, channels)[:total_rows]

    updates = pl.pallas_call(
        update_kernel,
        out_shape=tuple(shape(w.shape, F32) for w in weights) + (shape(loss.shape, F32),),
        in_specs=vmem(2),
        out_specs=tuple(vmem(5)),
        compiler_params=params,
        name="updates",
    )(whole, loss)
    return (*updates[:3], updates[3].T, updates[4][None])


def solution(mesh):
    in_specs = (P("rep", "vol", None), P("rep", "vol"), P("rep", None), P(), P(), P(), P())
    out_specs = (P(), P(), P(), P(), P("rep", "vol", None))
    return jax.shard_map(
        on_device, mesh=mesh, in_specs=in_specs, out_specs=out_specs, check_vma=False
    )
```

```python
import jax
import jax.numpy as jnp
from jax import lax
from jax.experimental import pallas as pl
from jax.experimental.pallas import tpu as pltpu
from jax.sharding import PartitionSpec as P

TEMPERATURE = 0.2
NORM_EPS = 1e-06
RMS_EPS = 1e-06
BF16 = jnp.bfloat16
F32 = jnp.float32
GROUP = 16


def nn(left, right):
    return lax.dot_general(left, right, (((1,), (0,)), ((), ())), preferred_element_type=F32)


def nt(left, right):
    return lax.dot_general(left, right, (((1,), (1,)), ((), ())), preferred_element_type=F32)


def tn(left, right):
    return lax.dot_general(left, right, (((0,), (0,)), ((), ())), preferred_element_type=F32)


def split(value):
    high = value.astype(BF16)
    low = (value - high.astype(F32)).astype(BF16)
    return high, low


def paired(weight):
    zero = jnp.zeros_like(weight)
    return jnp.concatenate(
        [
            jnp.concatenate([weight, zero], axis=1),
            jnp.concatenate([zero, weight], axis=1),
        ],
        axis=0,
    )


def pair_rows(cut_ref, width, first, number):
    return jnp.concatenate(
        [cut_ref[:, (first + i) * width : (first + i + 1) * width] for i in range(number)], axis=0
    )


def first_kernel(first_ref):
    first_ref[...] = jnp.zeros(first_ref.shape, first_ref.dtype)


def forward_kernel(
    first_ref, count_ref, cut_ref, stem_ref, mix_ref, out_in, proj_in, partner_hbm,
    send_ref, pooled_ref, mixed_ref, unit_ref, inv_ref, hidden_t_ref, patch_t_ref,
    stem_slope_ref, mix_slope_ref, mate_ref, half_mix_ref, out_ref, proj_ref,
    partner_ref, sem,
):
    nodes = cut_ref.shape[0]
    voxels, channels = stem_ref.shape
    width = 2 * voxels
    blocks = cut_ref.shape[1] // width
    del first_ref
    out_ref[...] = out_in[...]
    proj_ref[...] = proj_in[...]
    partner_copy = pltpu.make_async_copy(partner_hbm, partner_ref, sem)

    def begin(step, carry):
        @pl.when(step == 0)
        def _():
            partner_copy.start()

        return carry

    lax.fori_loop(0, 2, begin, 0)
    stem2 = paired((stem_ref[...].astype(F32) * 0.5).astype(BF16))
    mix2 = paired((mix_ref[...].astype(F32) * 0.5).astype(BF16))
    half_mix_ref[...] = mix2
    hidden_sum = jnp.zeros((nodes, 2 * channels), F32)
    mixed_sum = jnp.zeros((nodes, 2 * channels), F32)
    for first in range(0, blocks, GROUP):
        number = min(GROUP, blocks - first)
        rows = slice(first * nodes, (first + number) * nodes)
        patches = pair_rows(cut_ref, width, first, number)
        half = nn(patches, stem2)
        t = jnp.tanh(half)
        u = 1.0 + t
        hidden = half * u
        stem_slope_ref[rows, :] = u + hidden * (1.0 - t)
        narrow = hidden.astype(BF16)
        half = nn(narrow, mix2)
        t = jnp.tanh(half)
        u = 1.0 + t
        mixed = half * u
        mix_slope_ref[rows, :] = u + mixed * (1.0 - t)
        for i in range(number):
            part = slice(i * nodes, (i + 1) * nodes)
            hidden_sum = hidden_sum + hidden[part]
            mixed_sum = mixed_sum + mixed[part]
        hidden_t_ref[:, rows] = narrow.T
        patch_t_ref[:, rows] = patches.T
    hidden_sum = hidden_sum[:, :channels] + hidden_sum[:, channels:]
    mixed_sum = mixed_sum[:, :channels] + mixed_sum[:, channels:]
    high, low = split(mixed_sum)
    weight = out_ref[...]
    summed = hidden_sum + (nn(high, weight) + nn(low, weight))
    pooled = (summed / (2 * blocks)).astype(BF16)
    raw = nt(pooled, proj_ref[...])
    inv = lax.rsqrt(jnp.sum(raw * raw, axis=1, keepdims=True) + NORM_EPS)
    unit = raw * inv
    count = count_ref[0, 0]
    live = lax.broadcasted_iota(jnp.int32, unit.shape, 0) < count
    embed = jnp.where(live, unit, 0.0)
    counts = jnp.zeros(unit.shape, F32) + count.astype(F32)
    send = jnp.concatenate([embed, counts], axis=1).astype(BF16)
    send_ref[...] = jnp.broadcast_to(send[None], send_ref.shape)
    pooled_ref[...] = pooled
    mixed_ref[...] = mixed_sum
    unit_ref[...] = unit
    inv_ref[...] = inv

    partner_copy.wait()
    mate_ref[...] = partner_ref[...].astype(F32)


def slot_tables(gathered_ref, embed_dim, max_nodes):
    slots = gathered_ref.shape[0]
    owners = slots // max_nodes
    counts = jnp.concatenate(
        [
            gathered_ref[i * max_nodes : i * max_nodes + 8, embed_dim : embed_dim + 1].astype(F32)[:1]
            for i in range(owners)
        ],
        axis=0,
    )
    owner = lax.broadcasted_iota(jnp.int32, (owners, slots), 0)
    slot_owner = lax.broadcasted_iota(jnp.int32, (owners, slots), 1) // max_nodes
    count = jnp.sum(jnp.where(owner == slot_owner, counts, 0.0), axis=0, keepdims=True)
    offset = jnp.sum(jnp.where(owner < slot_owner, counts, 0.0), axis=0, keepdims=True)
    return count, offset, counts


def score_sums(gathered_ref, embed_dim, max_nodes, live_row):
    slots = gathered_ref.shape[0]
    step = min(slots, 256)
    whole = gathered_ref[:, :embed_dim]

    def block(first, total):
        part = gathered_ref[pl.ds(first, step), :]
        scores = nt(part[:, :embed_dim], whole) / TEMPERATURE
        count = part[:, embed_dim : embed_dim + 1].astype(F32)
        row = lax.broadcasted_iota(jnp.int32, (step, 1), 0) + first
        live = (row % max_nodes).astype(F32) < count
        column = lax.broadcasted_iota(jnp.int32, scores.shape, 1)
        keep = jnp.logical_and(live, column != row)
        return total + jnp.sum(jnp.where(keep, jnp.exp(scores), 0.0), axis=0, keepdims=True)

    total = jnp.zeros((1, slots), F32)
    if slots == step:
        total = block(0, total)
    else:
        total = lax.fori_loop(
            0, slots // step, lambda i, t: block(pl.multiple_of(i * step, step), t), total
        )
    return jnp.where(live_row, total, 1.0)


def look_up(table_ref, number):
    shape = (number.shape[0], table_ref.shape[1])
    listed = lax.broadcasted_iota(jnp.int32, shape, 1).astype(F32)
    return jnp.sum(jnp.where(listed == number, table_ref[...], 0.0), axis=1, keepdims=True)


def backward_kernel(
    gathered_ref, mate_ref, pooled_ref, mixed_ref, unit_ref, inv_ref,
    hidden_t_ref, patch_t_ref, stem_slope_ref, mix_slope_ref, half_mix_ref, out_ref, proj_ref,
    grad_ref, loss_ref,
):
    nodes, embed_dim = unit_ref.shape
    slots = gathered_ref.shape[0]
    place = lax.axis_index("vol")
    channels = out_ref.shape[0]
    voxels = patch_t_ref.shape[0] // 2
    blocks = stem_slope_ref.shape[0] // nodes

    count_row, offset_row, counts = slot_tables(gathered_ref, embed_dim, nodes)
    slot_row = lax.broadcasted_iota(jnp.int32, (1, slots), 1)
    within = (slot_row % nodes).astype(F32)
    live_row = within < count_row
    number_row = jnp.where(live_row, offset_row + within, -1.0)
    totals = score_sums(gathered_ref, embed_dim, nodes, live_row)

    owner = lax.broadcasted_iota(jnp.int32, counts.shape, 0)
    own_offset = jnp.sum(jnp.where(owner < place, counts, 0.0), axis=0, keepdims=True)
    rank = lax.broadcasted_iota(jnp.int32, (nodes, 1), 0)
    own_number = own_offset + rank.astype(F32)
    mate = look_up(mate_ref, own_number)
    companion = jnp.where(number_row == mate, 1.0, 0.0).astype(BF16)

    whole = gathered_ref[:, :embed_dim]
    own = gathered_ref[pl.ds(pl.multiple_of(place * nodes, nodes), nodes), :]
    own_live = rank.astype(F32) < own[:, embed_dim : embed_dim + 1].astype(F32)
    scores = nt(own[:, :embed_dim], whole) / TEMPERATURE
    other = jnp.logical_and(live_row, slot_row != rank + place * nodes)
    weight = jnp.where(other, jnp.exp(scores), 0.0)
    own_total = jnp.sum(weight, axis=1, keepdims=True)
    row_weight = (weight * (1.0 / own_total)).astype(BF16)
    column_weight = (weight * (1.0 / totals)).astype(BF16)
    mixed_rows = nn(jnp.concatenate([row_weight, column_weight, companion], axis=0), whole)
    d_embed = (
        mixed_rows[:nodes] + mixed_rows[nodes : 2 * nodes] - 2.0 * mixed_rows[2 * nodes :]
    ) / TEMPERATURE

    node_dev = loss_ref.shape[1]
    owners = slots // nodes
    wanted = (lax.broadcasted_iota(jnp.int32, (node_dev, 1), 0) * owners + place).astype(F32)
    mine = number_row == wanted
    total = jnp.sum(jnp.where(mine, totals, 0.0), axis=1, keepdims=True)
    anchor = nn(jnp.where(mine, 1.0, 0.0).astype(BF16), whole)
    other_end = number_row == look_up(mate_ref, wanted)
    other_end = nn(jnp.where(other_end, 1.0, 0.0).astype(BF16), whole)
    loss = jnp.log(total) - jnp.sum(anchor * other_end, axis=1, keepdims=True) / TEMPERATURE
    row = lax.broadcasted_iota(jnp.int32, (node_dev, node_dev), 0)
    column = lax.broadcasted_iota(jnp.int32, (node_dev, node_dev), 1)
    loss_ref[...] = jnp.sum(jnp.where(row == column, loss, 0.0), axis=0, keepdims=True)

    unit = unit_ref[...]
    radial = jnp.sum(unit * d_embed, axis=1, keepdims=True)
    d_raw = jnp.where(own_live, inv_ref[...] * (d_embed - unit * radial), 0.0).astype(BF16)
    g_proj = tn(d_raw, pooled_ref[...])
    d_sum = (nn(d_raw, proj_ref[...]) / (2 * blocks)).astype(BF16)
    high, low = split(mixed_ref[...])
    g_out = tn(high, d_sum) + tn(low, d_sum)
    d_mixed = 0.5 * nt(d_sum, out_ref[...])
    d_mixed = jnp.concatenate([d_mixed, d_mixed], axis=1)
    d_pool = 0.5 * d_sum.astype(F32)
    d_pool = jnp.concatenate([d_pool, d_pool], axis=1)
    half_mix = half_mix_ref[...]

    g_mix = jnp.zeros((2 * channels, 2 * channels), F32)
    g_stem = jnp.zeros((2 * voxels, 2 * channels), F32)
    chunk = 2 * GROUP
    for first in range(0, blocks, chunk):
        number = min(chunk, blocks - first)
        rows = slice(first * nodes, (first + number) * nodes)
        d_pre_mix = jnp.concatenate(
            [
                (d_mixed * mix_slope_ref[(first + i) * nodes : (first + i + 1) * nodes, :]).astype(BF16)
                for i in range(number)
            ],
            axis=0,
        )
        g_mix = g_mix + nn(hidden_t_ref[:, rows], d_pre_mix)
        back = nt(d_pre_mix, half_mix)
        d_pre_stem = jnp.concatenate(
            [
                (
                    (d_pool + back[i * nodes : (i + 1) * nodes])
                    * stem_slope_ref[(first + i) * nodes : (first + i + 1) * nodes, :]
                ).astype(BF16)
                for i in range(number)
            ],
            axis=0,
        )
        g_stem = g_stem + nn(patch_t_ref[:, rows], d_pre_stem)
    g_mix = g_mix[:channels, :channels] + g_mix[channels:, channels:]
    g_stem = g_stem[:voxels, :channels] + g_stem[voxels:, channels:]
    grads = jnp.concatenate([g_stem, g_mix, g_out, g_proj], axis=0)
    grad_ref[...] = grads.reshape(grad_ref.shape).astype(grad_ref.dtype)


def share_kernel(part_ref, send_ref, *, devices):
    parts = part_ref[...].astype(F32)
    total = jnp.sum(parts.reshape((devices, -1) + parts.shape[1:]), axis=0, keepdims=True)
    total = jnp.broadcast_to(total.astype(send_ref.dtype), (devices,) + total.shape[1:])
    send_ref[...] = total.reshape(send_ref.shape)


def update_kernel(grad_ref, own_loss_ref, *refs):
    *refs, loss_ref = refs
    loss_ref[...] = own_loss_ref[...]
    value = grad_ref[...].astype(F32).reshape(-1, grad_ref.shape[-1])
    start = 0
    for ref in refs:
        rows = ref.shape[0]
        grad = value[start : start + rows]
        start += rows
        squares = jnp.sum(jnp.sum(grad * grad, axis=0, keepdims=True), axis=1, keepdims=True)
        ref[...] = grad * lax.rsqrt(squares / (rows * ref.shape[1]) + RMS_EPS)


def vmem(number):
    return [pl.BlockSpec(memory_space=pltpu.VMEM)] * number


def hbm(number):
    return [pl.BlockSpec(memory_space=pltpu.HBM)] * number


def on_device(cutouts, counts, partner, w_stem, w_mix, w_out, w_proj):
    axes = ("vol", "rep")
    owners = lax.axis_size("vol")
    devices = owners * lax.axis_size("rep")
    cut = cutouts[0]
    nodes = cut.shape[0]
    voxels, channels = w_stem.shape
    embed_dim = w_proj.shape[1]
    rows = cut.shape[1] // (2 * voxels) * nodes
    w_proj = w_proj.T
    weights = (w_stem, w_mix, w_out, w_proj)
    shape = jax.ShapeDtypeStruct
    params = pltpu.CompilerParams(vmem_limit_bytes=(16 << 20) + owners * nodes * 8192)

    first = pl.pallas_call(
        first_kernel,
        out_shape=shape((8, 128), F32),
        out_specs=vmem(1)[0],
        compiler_params=params,
        cost_estimate=pl.CostEstimate(flops=10**9, transcendentals=10**6, bytes_accessed=10**8),
        name="first",
    )()
    send, *saved = pl.pallas_call(
        forward_kernel,
        out_shape=(
            shape((owners, nodes, 2 * embed_dim), BF16),
            shape((nodes, channels), BF16),
            shape((nodes, channels), F32),
            shape((nodes, embed_dim), F32),
            shape((nodes, 1), F32),
            shape((2 * channels, rows), BF16),
            shape((2 * voxels, rows), BF16),
            shape((rows, 2 * channels), F32),
            shape((rows, 2 * channels), F32),
            shape(partner.shape, F32),
            shape((2 * channels, 2 * channels), BF16),
            shape(w_out.shape, BF16),
            shape(w_proj.shape, BF16),
        ),
        in_specs=vmem(1) + [pl.BlockSpec(memory_space=pltpu.SMEM)] + vmem(5) + hbm(1),
        out_specs=tuple(vmem(13)),
        scratch_shapes=[pltpu.VMEM(partner.shape, jnp.int32), pltpu.SemaphoreType.DMA(())],
        compiler_params=params,
        name="forward",
    )(first, counts, cut, *weights, pltpu.with_memory_space_constraint(partner, pltpu.HBM))
    pooled, mixed_sum, unit, inv, hidden_t, patch_t, stem_slope, mix_slope, mates, *rest = saved

    gathered = lax.all_to_all(send, "vol", 0, 0).reshape(owners * nodes, 2 * embed_dim)

    total_rows = sum(w.shape[0] for w in weights)
    share = (total_rows + devices - 1) // devices
    tile = next(t for t in (8, 4, 2, 1) if share % t == 0)
    padded = share * devices - total_rows
    parts, loss = pl.pallas_call(
        backward_kernel,
        out_shape=(
            shape((total_rows, channels) if padded else (total_rows // tile, tile, channels), BF16),
            shape((1, partner.shape[1] // owners), F32),
        ),
        in_specs=vmem(13),
        out_specs=tuple(vmem(2)),
        compiler_params=params,
        name="backward",
    )(
        gathered, mates, pooled, mixed_sum, unit, inv,
        hidden_t, patch_t, stem_slope, mix_slope, *rest,
    )
    if padded:
        parts = jnp.pad(parts, ((0, padded), (0, 0))).reshape(-1, tile, channels)
    parts = lax.all_to_all(parts, axes, 0, 0, tiled=True)
    whole = pl.pallas_call(
        lambda *refs: share_kernel(*refs, devices=devices),
        out_shape=shape(parts.shape, BF16),
        in_specs=vmem(1),
        out_specs=vmem(1)[0],
        compiler_params=params,
        name="share",
    )(parts)
    whole = lax.all_to_all(whole, axes, 0, 0, tiled=True)
    if padded:
        whole = whole.reshape(-1, channels)[:total_rows]

    updates = pl.pallas_call(
        update_kernel,
        out_shape=tuple(shape(w.shape, F32) for w in weights) + (shape(loss.shape, F32),),
        in_specs=vmem(2),
        out_specs=tuple(vmem(5)),
        compiler_params=params,
        name="updates",
    )(whole, loss)
    return (*updates[:3], updates[3].T, updates[4][None])


def solution(mesh):
    in_specs = (P("rep", "vol", None), P("rep", "vol"), P("rep", None), P(), P(), P(), P())
    out_specs = (P(), P(), P(), P(), P("rep", "vol", None))
    return jax.shard_map(
        on_device, mesh=mesh, in_specs=in_specs, out_specs=out_specs, check_vma=False
    )
```

```python
import jax
import jax.numpy as jnp
from jax import lax
from jax.experimental import pallas as pl
from jax.experimental.pallas import tpu as pltpu
from jax.sharding import PartitionSpec as P

TEMPERATURE = 0.2
NORM_EPS = 1e-06
RMS_EPS = 1e-06
BF16 = jnp.bfloat16
F32 = jnp.float32
UNUSED = 2.0
GROUP = 16


def nn(left, right):
    return lax.dot_general(left, right, (((1,), (0,)), ((), ())), preferred_element_type=F32)


def nt(left, right):
    return lax.dot_general(left, right, (((1,), (1,)), ((), ())), preferred_element_type=F32)


def tn(left, right):
    return lax.dot_general(left, right, (((0,), (0,)), ((), ())), preferred_element_type=F32)


def split(value):
    high = value.astype(BF16)
    low = (value - high.astype(F32)).astype(BF16)
    return high, low


def paired(weight):
    zero = jnp.zeros_like(weight)
    return jnp.concatenate(
        [
            jnp.concatenate([weight, zero], axis=1),
            jnp.concatenate([zero, weight], axis=1),
        ],
        axis=0,
    )


def pair_rows(cut_ref, width, first, number):
    return jnp.concatenate(
        [cut_ref[:, (first + i) * width : (first + i + 1) * width] for i in range(number)], axis=0
    )


def first_kernel(first_ref):
    first_ref[...] = jnp.zeros(first_ref.shape, first_ref.dtype)


def forward_kernel(
    first_ref, count_ref, cut_ref, stem_ref, mix_ref, out_in, proj_in, partner_hbm,
    send_ref, pooled_ref, mixed_ref, unit_ref, inv_ref, hidden_t_ref, patch_t_ref,
    stem_slope_ref, mix_slope_ref, mate_ref, half_mix_ref, out_ref, proj_ref,
    partner_ref, sem,
):
    nodes = cut_ref.shape[0]
    voxels, channels = stem_ref.shape
    width = 2 * voxels
    blocks = cut_ref.shape[1] // width
    del first_ref
    out_ref[...] = out_in[...]
    proj_ref[...] = proj_in[...]
    partner_copy = pltpu.make_async_copy(partner_hbm, partner_ref, sem)

    def begin(step, carry):
        @pl.when(step == 0)
        def _():
            partner_copy.start()

        return carry

    lax.fori_loop(0, 2, begin, 0)
    stem2 = paired((stem_ref[...].astype(F32) * 0.5).astype(BF16))
    mix2 = paired((mix_ref[...].astype(F32) * 0.5).astype(BF16))
    half_mix_ref[...] = mix2
    hidden_sum = jnp.zeros((nodes, 2 * channels), F32)
    mixed_sum = jnp.zeros((nodes, 2 * channels), F32)
    for first in range(0, blocks, GROUP):
        number = min(GROUP, blocks - first)
        rows = slice(first * nodes, (first + number) * nodes)
        patches = pair_rows(cut_ref, width, first, number)
        half = nn(patches, stem2)
        t = jnp.tanh(half)
        u = 1.0 + t
        hidden = half * u
        stem_slope_ref[rows, :] = u + hidden * (1.0 - t)
        narrow = hidden.astype(BF16)
        half = nn(narrow, mix2)
        t = jnp.tanh(half)
        u = 1.0 + t
        mixed = half * u
        mix_slope_ref[rows, :] = u + mixed * (1.0 - t)
        for i in range(number):
            part = slice(i * nodes, (i + 1) * nodes)
            hidden_sum = hidden_sum + hidden[part]
            mixed_sum = mixed_sum + mixed[part]
        hidden_t_ref[:, rows] = narrow.T
        patch_t_ref[:, rows] = patches.T
    hidden_sum = hidden_sum[:, :channels] + hidden_sum[:, channels:]
    mixed_sum = mixed_sum[:, :channels] + mixed_sum[:, channels:]
    high, low = split(mixed_sum)
    weight = out_ref[...]
    summed = hidden_sum + (nn(high, weight) + nn(low, weight))
    pooled = (summed / (2 * blocks)).astype(BF16)
    raw = nt(pooled, proj_ref[...])
    inv = lax.rsqrt(jnp.sum(raw * raw, axis=1, keepdims=True) + NORM_EPS)
    unit = raw * inv
    count = count_ref[0, 0]
    live = lax.broadcasted_iota(jnp.int32, (nodes, 1), 0) < count
    embed = jnp.where(live, unit, UNUSED)
    send = jnp.concatenate([embed[: nodes // 2], embed[nodes // 2 :]], axis=1).astype(BF16)
    send_ref[...] = jnp.broadcast_to(send[None], send_ref.shape)
    pooled_ref[...] = pooled
    mixed_ref[...] = mixed_sum
    unit_ref[...] = unit
    inv_ref[...] = jnp.where(live, inv, 0.0)

    partner_copy.wait()
    mate_ref[...] = partner_ref[...].astype(F32)


def unpack(gathered_ref, whole_ref, max_nodes):
    slots, embed_dim = whole_ref.shape
    half = max_nodes // 2
    owners = slots // max_nodes
    whole_ref[: slots // 2, :] = gathered_ref[:, :embed_dim]
    whole_ref[slots // 2 :, :] = gathered_ref[:, embed_dim:]
    counts = []
    for owner in range(owners):
        used = gathered_ref[owner * half : (owner + 1) * half, :].astype(F32) < 0.75 * UNUSED
        counts.append(jnp.sum(jnp.where(used, 1.0, 0.0), axis=0, keepdims=True))
    counts = jnp.concatenate(counts, axis=0)
    counts = counts[:, 0:1] + counts[:, embed_dim : embed_dim + 1]
    owner = lax.broadcasted_iota(jnp.int32, (owners, slots), 0)
    slot = lax.broadcasted_iota(jnp.int32, (owners, slots), 1)
    slot_owner = slot % (slots // 2) // half
    count = jnp.sum(jnp.where(owner == slot_owner, counts, 0.0), axis=0, keepdims=True)
    offset = jnp.sum(jnp.where(owner < slot_owner, counts, 0.0), axis=0, keepdims=True)
    slot = lax.broadcasted_iota(jnp.int32, (1, slots), 1)
    within = (slot // (slots // 2) * half + slot % half).astype(F32)
    return within, offset, within < count, counts


def score_sums(whole_ref, live_row):
    slots = whole_ref.shape[0]
    step = min(slots, 256)
    whole = whole_ref[...]

    def block(first, total):
        part = whole_ref[pl.ds(first, step), :]
        scores = nt(part, whole) / TEMPERATURE
        row = lax.broadcasted_iota(jnp.int32, (step, 1), 0) + first
        live = part[:, 0:1].astype(F32) < 0.75 * UNUSED
        column = lax.broadcasted_iota(jnp.int32, scores.shape, 1)
        keep = jnp.logical_and(live, column != row)
        return total + jnp.sum(jnp.where(keep, jnp.exp(scores), 0.0), axis=0, keepdims=True)

    total = jnp.zeros((1, slots), F32)
    if slots == step:
        total = block(0, total)
    else:
        total = lax.fori_loop(
            0, slots // step, lambda i, t: block(pl.multiple_of(i * step, step), t), total
        )
    return jnp.where(live_row, total, 1.0)


def look_up(table_ref, number):
    shape = (number.shape[0], table_ref.shape[1])
    listed = lax.broadcasted_iota(jnp.int32, shape, 1).astype(F32)
    return jnp.sum(jnp.where(listed == number, table_ref[...], 0.0), axis=1, keepdims=True)


def backward_kernel(
    gathered_ref, mate_ref, pooled_ref, mixed_ref, unit_ref, inv_ref,
    hidden_t_ref, patch_t_ref, stem_slope_ref, mix_slope_ref, half_mix_ref, out_ref, proj_ref,
    grad_ref, loss_ref, whole_ref,
):
    nodes, embed_dim = unit_ref.shape
    slots = whole_ref.shape[0]
    place = lax.axis_index("vol")
    channels = out_ref.shape[0]
    voxels = patch_t_ref.shape[0] // 2
    blocks = stem_slope_ref.shape[0] // nodes
    half = nodes // 2

    within, offset_row, live_row, counts = unpack(gathered_ref, whole_ref, nodes)
    number_row = jnp.where(live_row, offset_row + within, -1.0)
    totals = score_sums(whole_ref, live_row)

    owner = lax.broadcasted_iota(jnp.int32, counts.shape, 0)
    own_offset = jnp.sum(jnp.where(owner < place, counts, 0.0), axis=0, keepdims=True)
    rank = lax.broadcasted_iota(jnp.int32, (nodes, 1), 0)
    own_number = own_offset + rank.astype(F32)
    mate = look_up(mate_ref, own_number)
    companion = jnp.where(number_row == mate, 1.0, 0.0).astype(BF16)

    whole = whole_ref[...]
    unit = unit_ref[...]
    scores = nt(unit.astype(BF16), whole) / TEMPERATURE
    own_slot = rank // half * (slots // 2) + place * half + rank % half
    slot_row = lax.broadcasted_iota(jnp.int32, (1, slots), 1)
    other = jnp.logical_and(live_row, slot_row != own_slot)
    weight = jnp.where(other, jnp.exp(scores), 0.0)
    own_total = jnp.sum(weight, axis=1, keepdims=True)
    row_weight = (weight * (1.0 / own_total)).astype(BF16)
    column_weight = (weight * (1.0 / totals)).astype(BF16)
    mixed_rows = nn(jnp.concatenate([row_weight, column_weight, companion], axis=0), whole)
    d_embed = (
        mixed_rows[:nodes] + mixed_rows[nodes : 2 * nodes] - 2.0 * mixed_rows[2 * nodes :]
    ) / TEMPERATURE

    node_dev = loss_ref.shape[1]
    owners = slots // nodes
    wanted = (lax.broadcasted_iota(jnp.int32, (node_dev, 1), 0) * owners + place).astype(F32)
    mine = number_row == wanted
    total = jnp.sum(jnp.where(mine, totals, 0.0), axis=1, keepdims=True)
    anchor = nn(jnp.where(mine, 1.0, 0.0).astype(BF16), whole)
    other_end = number_row == look_up(mate_ref, wanted)
    other_end = nn(jnp.where(other_end, 1.0, 0.0).astype(BF16), whole)
    loss = jnp.log(total) - jnp.sum(anchor * other_end, axis=1, keepdims=True) / TEMPERATURE
    row = lax.broadcasted_iota(jnp.int32, (node_dev, node_dev), 0)
    column = lax.broadcasted_iota(jnp.int32, (node_dev, node_dev), 1)
    loss_ref[...] = jnp.sum(jnp.where(row == column, loss, 0.0), axis=0, keepdims=True)

    radial = jnp.sum(unit * d_embed, axis=1, keepdims=True)
    d_raw = (inv_ref[...] * (d_embed - unit * radial)).astype(BF16)
    g_proj = tn(d_raw, pooled_ref[...])
    d_sum = (nn(d_raw, proj_ref[...]) / (2 * blocks)).astype(BF16)
    high, low = split(mixed_ref[...])
    g_out = tn(high, d_sum) + tn(low, d_sum)
    d_mixed = 0.5 * nt(d_sum, out_ref[...])
    d_mixed = jnp.concatenate([d_mixed, d_mixed], axis=1)
    d_pool = 0.5 * d_sum.astype(F32)
    d_pool = jnp.concatenate([d_pool, d_pool], axis=1)
    half_mix = half_mix_ref[...]

    g_mix = jnp.zeros((2 * channels, 2 * channels), F32)
    g_stem = jnp.zeros((2 * voxels, 2 * channels), F32)
    chunk = 2 * GROUP
    for first in range(0, blocks, chunk):
        number = min(chunk, blocks - first)
        rows = slice(first * nodes, (first + number) * nodes)
        d_pre_mix = jnp.concatenate(
            [
                (d_mixed * mix_slope_ref[(first + i) * nodes : (first + i + 1) * nodes, :]).astype(BF16)
                for i in range(number)
            ],
            axis=0,
        )
        g_mix = g_mix + nn(hidden_t_ref[:, rows], d_pre_mix)
        back = nt(d_pre_mix, half_mix)
        d_pre_stem = jnp.concatenate(
            [
                (
                    (d_pool + back[i * nodes : (i + 1) * nodes])
                    * stem_slope_ref[(first + i) * nodes : (first + i + 1) * nodes, :]
                ).astype(BF16)
                for i in range(number)
            ],
            axis=0,
        )
        g_stem = g_stem + nn(patch_t_ref[:, rows], d_pre_stem)
    g_mix = g_mix[:channels, :channels] + g_mix[channels:, channels:]
    g_stem = g_stem[:voxels, :channels] + g_stem[voxels:, channels:]
    grads = jnp.concatenate([g_stem, g_mix, g_out, g_proj], axis=0)
    grad_ref[...] = grads.reshape(grad_ref.shape).astype(grad_ref.dtype)


def share_kernel(part_ref, send_ref, *, devices):
    parts = part_ref[...].astype(F32)
    total = jnp.sum(parts.reshape((devices, -1) + parts.shape[1:]), axis=0, keepdims=True)
    total = jnp.broadcast_to(total.astype(send_ref.dtype), (devices,) + total.shape[1:])
    send_ref[...] = total.reshape(send_ref.shape)


def update_kernel(grad_ref, own_loss_ref, *refs):
    *refs, loss_ref = refs
    loss_ref[...] = own_loss_ref[...]
    value = grad_ref[...].astype(F32).reshape(-1, grad_ref.shape[-1])
    start = 0
    for ref in refs:
        rows = ref.shape[0]
        grad = value[start : start + rows]
        start += rows
        squares = jnp.sum(jnp.sum(grad * grad, axis=0, keepdims=True), axis=1, keepdims=True)
        ref[...] = grad * lax.rsqrt(squares / (rows * ref.shape[1]) + RMS_EPS)


def vmem(number):
    return [pl.BlockSpec(memory_space=pltpu.VMEM)] * number


def hbm(number):
    return [pl.BlockSpec(memory_space=pltpu.HBM)] * number


def on_device(cutouts, counts, partner, w_stem, w_mix, w_out, w_proj):
    axes = ("vol", "rep")
    owners = lax.axis_size("vol")
    devices = owners * lax.axis_size("rep")
    cut = cutouts[0]
    nodes = cut.shape[0]
    voxels, channels = w_stem.shape
    embed_dim = w_proj.shape[1]
    rows = cut.shape[1] // (2 * voxels) * nodes
    w_proj = w_proj.T
    weights = (w_stem, w_mix, w_out, w_proj)
    shape = jax.ShapeDtypeStruct
    params = pltpu.CompilerParams(vmem_limit_bytes=(16 << 20) + owners * nodes * 8192)

    first = pl.pallas_call(
        first_kernel,
        out_shape=shape((8, 128), F32),
        out_specs=vmem(1)[0],
        compiler_params=params,
        cost_estimate=pl.CostEstimate(flops=10**9, transcendentals=10**6, bytes_accessed=10**8),
        name="first",
    )()
    send, *saved = pl.pallas_call(
        forward_kernel,
        out_shape=(
            shape((owners, nodes // 2, 2 * embed_dim), BF16),
            shape((nodes, channels), BF16),
            shape((nodes, channels), F32),
            shape((nodes, embed_dim), F32),
            shape((nodes, 1), F32),
            shape((2 * channels, rows), BF16),
            shape((2 * voxels, rows), BF16),
            shape((rows, 2 * channels), F32),
            shape((rows, 2 * channels), F32),
            shape(partner.shape, F32),
            shape((2 * channels, 2 * channels), BF16),
            shape(w_out.shape, BF16),
            shape(w_proj.shape, BF16),
        ),
        in_specs=vmem(1) + [pl.BlockSpec(memory_space=pltpu.SMEM)] + vmem(5) + hbm(1),
        out_specs=tuple(vmem(13)),
        scratch_shapes=[pltpu.VMEM(partner.shape, jnp.int32), pltpu.SemaphoreType.DMA(())],
        compiler_params=params,
        name="forward",
    )(first, counts, cut, *weights, pltpu.with_memory_space_constraint(partner, pltpu.HBM))
    pooled, mixed_sum, unit, inv, hidden_t, patch_t, stem_slope, mix_slope, mates, *rest = saved

    gathered = lax.all_to_all(send, "vol", 0, 0).reshape(owners * nodes // 2, 2 * embed_dim)

    total_rows = sum(w.shape[0] for w in weights)
    share = (total_rows + devices - 1) // devices
    tile = next(t for t in (8, 4, 2, 1) if share % t == 0)
    padded = share * devices - total_rows
    parts, loss = pl.pallas_call(
        backward_kernel,
        out_shape=(
            shape((total_rows, channels) if padded else (total_rows // tile, tile, channels), BF16),
            shape((1, partner.shape[1] // owners), F32),
        ),
        in_specs=vmem(13),
        out_specs=tuple(vmem(2)),
        scratch_shapes=[pltpu.VMEM((owners * nodes, embed_dim), BF16)],
        compiler_params=params,
        name="backward",
    )(
        gathered, mates, pooled, mixed_sum, unit, inv,
        hidden_t, patch_t, stem_slope, mix_slope, *rest,
    )
    if padded:
        parts = jnp.pad(parts, ((0, padded), (0, 0))).reshape(-1, tile, channels)
    parts = lax.all_to_all(parts, axes, 0, 0, tiled=True)
    whole = pl.pallas_call(
        lambda *refs: share_kernel(*refs, devices=devices),
        out_shape=shape(parts.shape, BF16),
        in_specs=vmem(1),
        out_specs=vmem(1)[0],
        compiler_params=params,
        name="share",
    )(parts)
    whole = lax.all_to_all(whole, axes, 0, 0, tiled=True)
    if padded:
        whole = whole.reshape(-1, channels)[:total_rows]

    updates = pl.pallas_call(
        update_kernel,
        out_shape=tuple(shape(w.shape, F32) for w in weights) + (shape(loss.shape, F32),),
        in_specs=vmem(2),
        out_specs=tuple(vmem(5)),
        compiler_params=params,
        name="updates",
    )(whole, loss)
    return (*updates[:3], updates[3].T, updates[4][None])


def solution(mesh):
    in_specs = (P("rep", "vol", None), P("rep", "vol"), P("rep", None), P(), P(), P(), P())
    out_specs = (P(), P(), P(), P(), P("rep", "vol", None))
    return jax.shard_map(
        on_device, mesh=mesh, in_specs=in_specs, out_specs=out_specs, check_vma=False
    )
```

```python
import jax
import jax.numpy as jnp
from jax import lax
from jax.experimental import pallas as pl
from jax.experimental.pallas import tpu as pltpu
from jax.sharding import PartitionSpec as P

TEMPERATURE = 0.2
NORM_EPS = 1e-06
RMS_EPS = 1e-06
BF16 = jnp.bfloat16
F32 = jnp.float32
UNUSED = 2.0
GROUP = 16


def nn(left, right):
    return lax.dot_general(left, right, (((1,), (0,)), ((), ())), preferred_element_type=F32)


def nt(left, right):
    return lax.dot_general(left, right, (((1,), (1,)), ((), ())), preferred_element_type=F32)


def tn(left, right):
    return lax.dot_general(left, right, (((0,), (0,)), ((), ())), preferred_element_type=F32)


def split(value):
    high = value.astype(BF16)
    low = (value - high.astype(F32)).astype(BF16)
    return high, low


def paired(weight):
    zero = jnp.zeros_like(weight)
    return jnp.concatenate(
        [
            jnp.concatenate([weight, zero], axis=1),
            jnp.concatenate([zero, weight], axis=1),
        ],
        axis=0,
    )


def pair_rows(cut_ref, width, first, number):
    return jnp.concatenate(
        [cut_ref[:, (first + i) * width : (first + i + 1) * width] for i in range(number)], axis=0
    )


def first_kernel(first_ref):
    first_ref[...] = jnp.zeros(first_ref.shape, first_ref.dtype)


def forward_kernel(
    first_ref, count_ref, cut_ref, stem_ref, mix_ref, out_in, proj_in, partner_hbm,
    send_ref, pooled_ref, mixed_ref, unit_ref, inv_ref, hidden_t_ref, patch_t_ref,
    stem_slope_ref, mix_slope_ref, mate_ref, half_mix_ref, out_ref, proj_ref,
    partner_ref, sem,
):
    nodes = cut_ref.shape[0]
    voxels, channels = stem_ref.shape
    width = 2 * voxels
    blocks = cut_ref.shape[1] // width
    del first_ref
    out_ref[...] = out_in[...]
    proj_ref[...] = proj_in[...]
    partner_copy = pltpu.make_async_copy(partner_hbm, partner_ref, sem)

    def begin(step, carry):
        @pl.when(step == 0)
        def _():
            partner_copy.start()

        return carry

    lax.fori_loop(0, 2, begin, 0)
    stem2 = paired((stem_ref[...].astype(F32) * 0.5).astype(BF16))
    mix2 = paired((mix_ref[...].astype(F32) * 0.5).astype(BF16))
    half_mix_ref[...] = mix2
    hidden_sum = jnp.zeros((nodes, 2 * channels), F32)
    mixed_sum = jnp.zeros((nodes, 2 * channels), F32)
    for first in range(0, blocks, GROUP):
        number = min(GROUP, blocks - first)
        rows = slice(first * nodes, (first + number) * nodes)
        patches = pair_rows(cut_ref, width, first, number)
        half = nn(patches, stem2)
        t = jnp.tanh(half)
        u = 1.0 + t
        hidden = half * u
        stem_slope_ref[rows, :] = u + hidden * (1.0 - t)
        narrow = hidden.astype(BF16)
        half = nn(narrow, mix2)
        t = jnp.tanh(half)
        u = 1.0 + t
        mixed = half * u
        mix_slope_ref[rows, :] = u + mixed * (1.0 - t)
        for i in range(number):
            part = slice(i * nodes, (i + 1) * nodes)
            hidden_sum = hidden_sum + hidden[part]
            mixed_sum = mixed_sum + mixed[part]
        hidden_t_ref[:, rows] = narrow.T
        patch_t_ref[:, rows] = patches.T
    hidden_sum = hidden_sum[:, :channels] + hidden_sum[:, channels:]
    mixed_sum = mixed_sum[:, :channels] + mixed_sum[:, channels:]
    high, low = split(mixed_sum)
    weight = out_ref[...]
    summed = hidden_sum + (nn(high, weight) + nn(low, weight))
    pooled = (summed / (2 * blocks)).astype(BF16)
    raw = nt(pooled, proj_ref[...])
    inv = lax.rsqrt(jnp.sum(raw * raw, axis=1, keepdims=True) + NORM_EPS)
    unit = raw * inv
    count = count_ref[0, 0]
    live = lax.broadcasted_iota(jnp.int32, (nodes, 1), 0) < count
    embed = jnp.where(live, unit, UNUSED)
    send = jnp.concatenate([embed[: nodes // 2], embed[nodes // 2 :]], axis=1).astype(BF16)
    send_ref[...] = jnp.broadcast_to(send[None], send_ref.shape)
    pooled_ref[...] = pooled
    mixed_ref[...] = mixed_sum
    unit_ref[...] = unit
    inv_ref[...] = jnp.where(live, inv, 0.0)

    partner_copy.wait()
    mate_ref[...] = partner_ref[...].astype(F32)


def unpack(gathered_ref, whole_ref, max_nodes):
    slots, embed_dim = whole_ref.shape
    half = max_nodes // 2
    owners = slots // max_nodes
    whole_ref[: slots // 2, :] = gathered_ref[:, :embed_dim]
    whole_ref[slots // 2 :, :] = gathered_ref[:, embed_dim:]
    counts = []
    for owner in range(owners):
        used = gathered_ref[owner * half : (owner + 1) * half, :].astype(F32) < 0.75 * UNUSED
        counts.append(jnp.sum(jnp.where(used, 1.0, 0.0), axis=0, keepdims=True))
    counts = jnp.concatenate(counts, axis=0)
    counts = counts[:, 0:1] + counts[:, embed_dim : embed_dim + 1]
    owner = lax.broadcasted_iota(jnp.int32, (owners, slots), 0)
    slot = lax.broadcasted_iota(jnp.int32, (owners, slots), 1)
    slot_owner = slot % (slots // 2) // half
    count = jnp.sum(jnp.where(owner == slot_owner, counts, 0.0), axis=0, keepdims=True)
    offset = jnp.sum(jnp.where(owner < slot_owner, counts, 0.0), axis=0, keepdims=True)
    slot = lax.broadcasted_iota(jnp.int32, (1, slots), 1)
    within = (slot // (slots // 2) * half + slot % half).astype(F32)
    return within, offset, within < count, counts


def score_sums(whole_ref, live_row):
    slots = whole_ref.shape[0]
    step = min(slots, 256)
    whole = whole_ref[...]

    def block(first, total):
        part = whole_ref[pl.ds(first, step), :]
        scores = nt(part, whole) / TEMPERATURE
        row = lax.broadcasted_iota(jnp.int32, (step, 1), 0) + first
        live = part[:, 0:1].astype(F32) < 0.75 * UNUSED
        column = lax.broadcasted_iota(jnp.int32, scores.shape, 1)
        keep = jnp.logical_and(live, column != row)
        return total + jnp.sum(jnp.where(keep, jnp.exp(scores), 0.0), axis=0, keepdims=True)

    total = jnp.zeros((1, slots), F32)
    if slots == step:
        total = block(0, total)
    else:
        total = lax.fori_loop(
            0, slots // step, lambda i, t: block(pl.multiple_of(i * step, step), t), total
        )
    return jnp.where(live_row, total, 1.0)


def look_up(table_ref, number):
    shape = (number.shape[0], table_ref.shape[1])
    listed = lax.broadcasted_iota(jnp.int32, shape, 1).astype(F32)
    return jnp.sum(jnp.where(listed == number, table_ref[...], 0.0), axis=1, keepdims=True)


def backward_kernel(
    gathered_ref, mate_ref, pooled_ref, mixed_ref, unit_ref, inv_ref,
    hidden_t_ref, patch_t_ref, stem_slope_ref, mix_slope_ref, half_mix_ref, out_ref, proj_ref,
    grad_ref, loss_ref, whole_ref,
):
    nodes, embed_dim = unit_ref.shape
    slots = whole_ref.shape[0]
    place = lax.axis_index("vol")
    channels = out_ref.shape[0]
    voxels = patch_t_ref.shape[0] // 2
    blocks = stem_slope_ref.shape[0] // nodes
    half = nodes // 2

    within, offset_row, live_row, counts = unpack(gathered_ref, whole_ref, nodes)
    number_row = jnp.where(live_row, offset_row + within, -1.0)
    totals = score_sums(whole_ref, live_row)

    owner = lax.broadcasted_iota(jnp.int32, counts.shape, 0)
    own_offset = jnp.sum(jnp.where(owner < place, counts, 0.0), axis=0, keepdims=True)
    rank = lax.broadcasted_iota(jnp.int32, (nodes, 1), 0)
    own_number = own_offset + rank.astype(F32)
    mate = look_up(mate_ref, own_number)
    companion = jnp.where(number_row == mate, 1.0, 0.0).astype(BF16)

    whole = whole_ref[...]
    unit = unit_ref[...]
    scores = nt(unit.astype(BF16), whole) / TEMPERATURE
    own_slot = rank // half * (slots // 2) + place * half + rank % half
    slot_row = lax.broadcasted_iota(jnp.int32, (1, slots), 1)
    other = jnp.logical_and(live_row, slot_row != own_slot)
    weight = jnp.where(other, jnp.exp(scores), 0.0)
    own_total = jnp.sum(weight, axis=1, keepdims=True)
    row_weight = (weight * (1.0 / own_total)).astype(BF16)
    column_weight = (weight * (1.0 / totals)).astype(BF16)
    mixed_rows = nn(jnp.concatenate([row_weight, column_weight, companion], axis=0), whole)
    d_embed = (
        mixed_rows[:nodes] + mixed_rows[nodes : 2 * nodes] - 2.0 * mixed_rows[2 * nodes :]
    ) / TEMPERATURE

    node_dev = loss_ref.shape[1]
    owners = slots // nodes
    wanted = (lax.broadcasted_iota(jnp.int32, (node_dev, 1), 0) * owners + place).astype(F32)
    mine = number_row == wanted
    total = jnp.sum(jnp.where(mine, totals, 0.0), axis=1, keepdims=True)
    anchor = nn(jnp.where(mine, 1.0, 0.0).astype(BF16), whole)
    other_end = number_row == look_up(mate_ref, wanted)
    other_end = nn(jnp.where(other_end, 1.0, 0.0).astype(BF16), whole)
    loss = jnp.log(total) - jnp.sum(anchor * other_end, axis=1, keepdims=True) / TEMPERATURE
    row = lax.broadcasted_iota(jnp.int32, (node_dev, node_dev), 0)
    column = lax.broadcasted_iota(jnp.int32, (node_dev, node_dev), 1)
    loss_ref[...] = jnp.sum(jnp.where(row == column, loss, 0.0), axis=0, keepdims=True)

    radial = jnp.sum(unit * d_embed, axis=1, keepdims=True)
    d_raw = (inv_ref[...] * (d_embed - unit * radial)).astype(BF16)
    g_proj = tn(d_raw, pooled_ref[...])
    d_sum = (nn(d_raw, proj_ref[...]) / (2 * blocks)).astype(BF16)
    high, low = split(mixed_ref[...])
    g_out = tn(high, d_sum) + tn(low, d_sum)
    d_mixed = 0.5 * nt(d_sum, out_ref[...])
    d_mixed = jnp.concatenate([d_mixed, d_mixed], axis=1)
    d_pool = 0.5 * d_sum.astype(F32)
    d_pool = jnp.concatenate([d_pool, d_pool], axis=1)
    half_mix = half_mix_ref[...]

    g_mix = jnp.zeros((2 * channels, 2 * channels), F32)
    g_stem = jnp.zeros((2 * voxels, 2 * channels), F32)
    chunk = 2 * GROUP
    for first in range(0, blocks, chunk):
        number = min(chunk, blocks - first)
        rows = slice(first * nodes, (first + number) * nodes)
        d_pre_mix = jnp.concatenate(
            [
                (d_mixed * mix_slope_ref[(first + i) * nodes : (first + i + 1) * nodes, :]).astype(BF16)
                for i in range(number)
            ],
            axis=0,
        )
        g_mix = g_mix + nn(hidden_t_ref[:, rows], d_pre_mix)
        back = nt(d_pre_mix, half_mix)
        d_pre_stem = jnp.concatenate(
            [
                (
                    (d_pool + back[i * nodes : (i + 1) * nodes])
                    * stem_slope_ref[(first + i) * nodes : (first + i + 1) * nodes, :]
                ).astype(BF16)
                for i in range(number)
            ],
            axis=0,
        )
        g_stem = g_stem + nn(patch_t_ref[:, rows], d_pre_stem)
    g_mix = g_mix[:channels, :channels] + g_mix[channels:, channels:]
    g_stem = g_stem[:voxels, :channels] + g_stem[voxels:, channels:]
    grads = jnp.concatenate([g_stem, g_mix, g_out, g_proj], axis=0)
    grad_ref[...] = grads.reshape(grad_ref.shape).astype(grad_ref.dtype)


def share_kernel(part_ref, send_ref, *, devices):
    parts = part_ref[...].astype(F32)
    total = jnp.sum(parts.reshape((devices, -1) + parts.shape[1:]), axis=0, keepdims=True)
    total = jnp.broadcast_to(total.astype(send_ref.dtype), (devices,) + total.shape[1:])
    send_ref[...] = total.reshape(send_ref.shape)


def update_kernel(grad_ref, own_loss_ref, *refs):
    *refs, loss_ref = refs
    loss_ref[...] = own_loss_ref[...]
    value = grad_ref[...].astype(F32).reshape(-1, grad_ref.shape[-1])
    start = 0
    for ref in refs:
        rows = ref.shape[0]
        grad = value[start : start + rows]
        start += rows
        squares = jnp.sum(jnp.sum(grad * grad, axis=0, keepdims=True), axis=1, keepdims=True)
        ref[...] = grad * lax.rsqrt(squares / (rows * ref.shape[1]) + RMS_EPS)


def vmem(number):
    return [pl.BlockSpec(memory_space=pltpu.VMEM)] * number


def hbm(number):
    return [pl.BlockSpec(memory_space=pltpu.HBM)] * number


def on_device(cutouts, counts, partner, w_stem, w_mix, w_out, w_proj):
    axes = ("rep", "vol")
    owners = lax.axis_size("vol")
    devices = owners * lax.axis_size("rep")
    cut = cutouts[0]
    nodes = cut.shape[0]
    voxels, channels = w_stem.shape
    embed_dim = w_proj.shape[1]
    rows = cut.shape[1] // (2 * voxels) * nodes
    w_proj = w_proj.T
    weights = (w_stem, w_mix, w_out, w_proj)
    shape = jax.ShapeDtypeStruct
    params = pltpu.CompilerParams(vmem_limit_bytes=(16 << 20) + owners * nodes * 8192)

    first = pl.pallas_call(
        first_kernel,
        out_shape=shape((8, 128), F32),
        out_specs=vmem(1)[0],
        compiler_params=params,
        cost_estimate=pl.CostEstimate(flops=10**9, transcendentals=10**6, bytes_accessed=10**8),
        name="first",
    )()
    send, *saved = pl.pallas_call(
        forward_kernel,
        out_shape=(
            shape((owners, nodes // 2, 2 * embed_dim), BF16),
            shape((nodes, channels), BF16),
            shape((nodes, channels), F32),
            shape((nodes, embed_dim), F32),
            shape((nodes, 1), F32),
            shape((2 * channels, rows), BF16),
            shape((2 * voxels, rows), BF16),
            shape((rows, 2 * channels), F32),
            shape((rows, 2 * channels), F32),
            shape(partner.shape, F32),
            shape((2 * channels, 2 * channels), BF16),
            shape(w_out.shape, BF16),
            shape(w_proj.shape, BF16),
        ),
        in_specs=vmem(1) + [pl.BlockSpec(memory_space=pltpu.SMEM)] + vmem(5) + hbm(1),
        out_specs=tuple(vmem(13)),
        scratch_shapes=[pltpu.VMEM(partner.shape, jnp.int32), pltpu.SemaphoreType.DMA(())],
        compiler_params=params,
        name="forward",
    )(first, counts, cut, *weights, pltpu.with_memory_space_constraint(partner, pltpu.HBM))
    pooled, mixed_sum, unit, inv, hidden_t, patch_t, stem_slope, mix_slope, mates, *rest = saved

    gathered = lax.all_to_all(send, "vol", 0, 0).reshape(owners * nodes // 2, 2 * embed_dim)

    total_rows = sum(w.shape[0] for w in weights)
    share = (total_rows + devices - 1) // devices
    tile = next(t for t in (8, 4, 2, 1) if share % t == 0)
    padded = share * devices - total_rows
    parts, loss = pl.pallas_call(
        backward_kernel,
        out_shape=(
            shape((total_rows, channels) if padded else (total_rows // tile, tile, channels), BF16),
            shape((1, partner.shape[1] // owners), F32),
        ),
        in_specs=vmem(13),
        out_specs=tuple(vmem(2)),
        scratch_shapes=[pltpu.VMEM((owners * nodes, embed_dim), BF16)],
        compiler_params=params,
        name="backward",
    )(
        gathered, mates, pooled, mixed_sum, unit, inv,
        hidden_t, patch_t, stem_slope, mix_slope, *rest,
    )
    if padded:
        parts = jnp.pad(parts, ((0, padded), (0, 0))).reshape(-1, tile, channels)
    parts = lax.all_to_all(parts, axes, 0, 0, tiled=True)
    whole = pl.pallas_call(
        lambda *refs: share_kernel(*refs, devices=devices),
        out_shape=shape(parts.shape, BF16),
        in_specs=vmem(1),
        out_specs=vmem(1)[0],
        compiler_params=params,
        name="share",
    )(parts)
    whole = lax.all_to_all(whole, axes, 0, 0, tiled=True)
    if padded:
        whole = whole.reshape(-1, channels)[:total_rows]

    updates = pl.pallas_call(
        update_kernel,
        out_shape=tuple(shape(w.shape, F32) for w in weights) + (shape(loss.shape, F32),),
        in_specs=vmem(2),
        out_specs=tuple(vmem(5)),
        compiler_params=params,
        name="updates",
    )(whole, loss)
    return (*updates[:3], updates[3].T, updates[4][None])


def solution(mesh):
    in_specs = (P("rep", "vol", None), P("rep", "vol"), P("rep", None), P(), P(), P(), P())
    out_specs = (P(), P(), P(), P(), P("rep", "vol", None))
    return jax.shard_map(
        on_device, mesh=mesh, in_specs=in_specs, out_specs=out_specs, check_vma=False
    )
```

```python
import jax
import jax.numpy as jnp
from jax import lax
from jax.experimental import pallas as pl
from jax.experimental.pallas import tpu as pltpu
from jax.sharding import PartitionSpec as P

TEMPERATURE = 0.2
NORM_EPS = 1e-06
RMS_EPS = 1e-06
BF16 = jnp.bfloat16
F32 = jnp.float32
UNUSED = 2.0
GROUP = 16


def nn(left, right):
    return lax.dot_general(left, right, (((1,), (0,)), ((), ())), preferred_element_type=F32)


def nt(left, right):
    return lax.dot_general(left, right, (((1,), (1,)), ((), ())), preferred_element_type=F32)


def tn(left, right):
    return lax.dot_general(left, right, (((0,), (0,)), ((), ())), preferred_element_type=F32)


def split(value):
    high = value.astype(BF16)
    low = (value - high.astype(F32)).astype(BF16)
    return high, low


def paired(weight):
    zero = jnp.zeros_like(weight)
    return jnp.concatenate(
        [
            jnp.concatenate([weight, zero], axis=1),
            jnp.concatenate([zero, weight], axis=1),
        ],
        axis=0,
    )


def pair_rows(cut_ref, width, first, number):
    return jnp.concatenate(
        [cut_ref[:, (first + i) * width : (first + i + 1) * width] for i in range(number)], axis=0
    )


def first_kernel(first_ref):
    first_ref[...] = jnp.zeros(first_ref.shape, first_ref.dtype)


def forward_kernel(
    first_ref, count_ref, cut_ref, stem_ref, mix_ref, out_in, proj_in, partner_hbm,
    send_ref, pooled_ref, mixed_ref, unit_ref, inv_ref, hidden_t_ref, patch_t_ref,
    stem_slope_ref, mix_slope_ref, mate_ref, half_mix_ref, out_ref, proj_ref,
    partner_ref, sem,
):
    nodes = cut_ref.shape[0]
    voxels, channels = stem_ref.shape
    width = 2 * voxels
    blocks = cut_ref.shape[1] // width
    del first_ref
    out_ref[...] = out_in[...]
    proj_ref[...] = proj_in[...]
    partner_copy = pltpu.make_async_copy(partner_hbm, partner_ref, sem)

    def begin(step, carry):
        @pl.when(step == 0)
        def _():
            partner_copy.start()

        return carry

    lax.fori_loop(0, 2, begin, 0)
    stem2 = paired((stem_ref[...].astype(F32) * 0.5).astype(BF16))
    mix2 = paired((mix_ref[...].astype(F32) * 0.5).astype(BF16))
    half_mix_ref[...] = mix2
    hidden_sum = jnp.zeros((nodes, 2 * channels), F32)
    mixed_sum = jnp.zeros((nodes, 2 * channels), F32)
    for first in range(0, blocks, GROUP):
        number = min(GROUP, blocks - first)
        rows = slice(first * nodes, (first + number) * nodes)
        patches = pair_rows(cut_ref, width, first, number)
        half = nn(patches, stem2)
        t = jnp.tanh(half)
        u = 1.0 + t
        hidden = half * u
        stem_slope_ref[rows, :] = u + hidden * (1.0 - t)
        narrow = hidden.astype(BF16)
        half = nn(narrow, mix2)
        t = jnp.tanh(half)
        u = 1.0 + t
        mixed = half * u
        mix_slope_ref[rows, :] = u + mixed * (1.0 - t)
        for i in range(number):
            part = slice(i * nodes, (i + 1) * nodes)
            hidden_sum = hidden_sum + hidden[part]
            mixed_sum = mixed_sum + mixed[part]
        hidden_t_ref[:, rows] = narrow.T
        patch_t_ref[:, rows] = patches.T
    hidden_sum = hidden_sum[:, :channels] + hidden_sum[:, channels:]
    mixed_sum = mixed_sum[:, :channels] + mixed_sum[:, channels:]
    high, low = split(mixed_sum)
    weight = out_ref[...]
    summed = hidden_sum + (nn(high, weight) + nn(low, weight))
    pooled = (summed / (2 * blocks)).astype(BF16)
    raw = nt(pooled, proj_ref[...])
    inv = lax.rsqrt(jnp.sum(raw * raw, axis=1, keepdims=True) + NORM_EPS)
    unit = raw * inv
    count = count_ref[0, 0]
    live = lax.broadcasted_iota(jnp.int32, (nodes, 1), 0) < count
    embed = jnp.where(live, unit, UNUSED)
    send = jnp.concatenate([embed[: nodes // 2], embed[nodes // 2 :]], axis=1).astype(BF16)
    send_ref[...] = jnp.broadcast_to(send[None], send_ref.shape)
    pooled_ref[...] = pooled
    mixed_ref[...] = mixed_sum
    unit_ref[...] = unit
    inv_ref[...] = jnp.where(live, inv, 0.0)

    partner_copy.wait()
    mate_ref[...] = partner_ref[...].astype(F32)


def unpack(gathered_ref, whole_ref, max_nodes):
    slots, embed_dim = whole_ref.shape
    half = max_nodes // 2
    owners = slots // max_nodes
    whole_ref[: slots // 2, :] = gathered_ref[:, :embed_dim]
    whole_ref[slots // 2 :, :] = gathered_ref[:, embed_dim:]
    counts = []
    for owner in range(owners):
        used = gathered_ref[owner * half : (owner + 1) * half, :].astype(F32) < 0.75 * UNUSED
        counts.append(jnp.sum(jnp.where(used, 1.0, 0.0), axis=0, keepdims=True))
    counts = jnp.concatenate(counts, axis=0)
    counts = counts[:, 0:1] + counts[:, embed_dim : embed_dim + 1]
    owner = lax.broadcasted_iota(jnp.int32, (owners, slots), 0)
    slot = lax.broadcasted_iota(jnp.int32, (owners, slots), 1)
    slot_owner = slot % (slots // 2) // half
    count = jnp.sum(jnp.where(owner == slot_owner, counts, 0.0), axis=0, keepdims=True)
    offset = jnp.sum(jnp.where(owner < slot_owner, counts, 0.0), axis=0, keepdims=True)
    slot = lax.broadcasted_iota(jnp.int32, (1, slots), 1)
    within = (slot // (slots // 2) * half + slot % half).astype(F32)
    return within, offset, within < count, counts


def score_sums(whole_ref, live_row):
    slots = whole_ref.shape[0]
    step = min(slots, 256)
    whole = whole_ref[...]

    def block(first, total):
        part = whole_ref[pl.ds(first, step), :]
        scores = nt(part, whole) / TEMPERATURE
        row = lax.broadcasted_iota(jnp.int32, (step, 1), 0) + first
        live = part[:, 0:1].astype(F32) < 0.75 * UNUSED
        column = lax.broadcasted_iota(jnp.int32, scores.shape, 1)
        keep = jnp.logical_and(live, column != row)
        return total + jnp.sum(jnp.where(keep, jnp.exp(scores), 0.0), axis=0, keepdims=True)

    total = jnp.zeros((1, slots), F32)
    if slots == step:
        total = block(0, total)
    else:
        total = lax.fori_loop(
            0, slots // step, lambda i, t: block(pl.multiple_of(i * step, step), t), total
        )
    return jnp.where(live_row, total, 1.0)


def look_up(table_ref, number):
    shape = (number.shape[0], table_ref.shape[1])
    listed = lax.broadcasted_iota(jnp.int32, shape, 1).astype(F32)
    return jnp.sum(jnp.where(listed == number, table_ref[...], 0.0), axis=1, keepdims=True)


def backward_kernel(
    gathered_ref, mate_ref, pooled_ref, mixed_ref, unit_ref, inv_ref,
    hidden_t_ref, patch_t_ref, stem_slope_ref, mix_slope_ref, half_mix_ref, out_ref, proj_ref,
    grad_ref, loss_ref, whole_ref,
):
    nodes, embed_dim = unit_ref.shape
    slots = whole_ref.shape[0]
    place = lax.axis_index("vol")
    channels = out_ref.shape[0]
    voxels = patch_t_ref.shape[0] // 2
    blocks = stem_slope_ref.shape[0] // nodes
    half = nodes // 2

    within, offset_row, live_row, counts = unpack(gathered_ref, whole_ref, nodes)
    number_row = jnp.where(live_row, offset_row + within, -1.0)
    totals = score_sums(whole_ref, live_row)

    owner = lax.broadcasted_iota(jnp.int32, counts.shape, 0)
    own_offset = jnp.sum(jnp.where(owner < place, counts, 0.0), axis=0, keepdims=True)
    rank = lax.broadcasted_iota(jnp.int32, (nodes, 1), 0)
    own_number = own_offset + rank.astype(F32)
    mate = look_up(mate_ref, own_number)
    companion = jnp.where(number_row == mate, 1.0, 0.0).astype(BF16)

    whole = whole_ref[...]
    unit = unit_ref[...]
    scores = nt(unit.astype(BF16), whole) / TEMPERATURE
    own_slot = rank // half * (slots // 2) + place * half + rank % half
    slot_row = lax.broadcasted_iota(jnp.int32, (1, slots), 1)
    other = jnp.logical_and(live_row, slot_row != own_slot)
    weight = jnp.where(other, jnp.exp(scores), 0.0)
    own_total = jnp.sum(weight, axis=1, keepdims=True)
    row_weight = (weight * (1.0 / own_total)).astype(BF16)
    column_weight = (weight * (1.0 / totals)).astype(BF16)
    mixed_rows = nn(jnp.concatenate([row_weight, column_weight, companion], axis=0), whole)
    d_embed = (
        mixed_rows[:nodes] + mixed_rows[nodes : 2 * nodes] - 2.0 * mixed_rows[2 * nodes :]
    ) / TEMPERATURE

    node_dev = loss_ref.shape[1]
    owners = slots // nodes
    wanted = (lax.broadcasted_iota(jnp.int32, (node_dev, 1), 0) * owners + place).astype(F32)
    mine = number_row == wanted
    total = jnp.sum(jnp.where(mine, totals, 0.0), axis=1, keepdims=True)
    anchor = nn(jnp.where(mine, 1.0, 0.0).astype(BF16), whole)
    other_end = number_row == look_up(mate_ref, wanted)
    other_end = nn(jnp.where(other_end, 1.0, 0.0).astype(BF16), whole)
    loss = jnp.log(total) - jnp.sum(anchor * other_end, axis=1, keepdims=True) / TEMPERATURE
    row = lax.broadcasted_iota(jnp.int32, (node_dev, node_dev), 0)
    column = lax.broadcasted_iota(jnp.int32, (node_dev, node_dev), 1)
    loss_ref[...] = jnp.sum(jnp.where(row == column, loss, 0.0), axis=0, keepdims=True)

    radial = jnp.sum(unit * d_embed, axis=1, keepdims=True)
    d_raw = (inv_ref[...] * (d_embed - unit * radial)).astype(BF16)
    d_sum = (nn(d_raw, proj_ref[...]) / (2 * blocks)).astype(BF16)
    high, low = split(mixed_ref[...])
    outer = tn(d_raw, jnp.concatenate([high, low, pooled_ref[...]], axis=1))
    g_out = outer[:, :channels] + outer[:, channels : 2 * channels]
    g_proj = outer[:, 2 * channels :]
    d_mixed = 0.5 * nt(d_sum, out_ref[...])
    d_mixed = jnp.concatenate([d_mixed, d_mixed], axis=1)
    d_pool = 0.5 * d_sum.astype(F32)
    d_pool = jnp.concatenate([d_pool, d_pool], axis=1)
    half_mix = half_mix_ref[...]

    g_mix = jnp.zeros((2 * channels, 2 * channels), F32)
    g_stem = jnp.zeros((2 * voxels, 2 * channels), F32)
    chunk = 2 * GROUP
    for first in range(0, blocks, chunk):
        number = min(chunk, blocks - first)
        rows = slice(first * nodes, (first + number) * nodes)
        d_pre_mix = jnp.concatenate(
            [
                (d_mixed * mix_slope_ref[(first + i) * nodes : (first + i + 1) * nodes, :]).astype(BF16)
                for i in range(number)
            ],
            axis=0,
        )
        g_mix = g_mix + nn(hidden_t_ref[:, rows], d_pre_mix)
        back = nt(d_pre_mix, half_mix)
        d_pre_stem = jnp.concatenate(
            [
                (
                    (d_pool + back[i * nodes : (i + 1) * nodes])
                    * stem_slope_ref[(first + i) * nodes : (first + i + 1) * nodes, :]
                ).astype(BF16)
                for i in range(number)
            ],
            axis=0,
        )
        g_stem = g_stem + nn(patch_t_ref[:, rows], d_pre_stem)
    g_mix = g_mix[:channels, :channels] + g_mix[channels:, channels:]
    g_stem = g_stem[:voxels, :channels] + g_stem[voxels:, channels:]
    grads = jnp.concatenate([g_stem, g_mix, g_out, g_proj], axis=0)
    grad_ref[...] = grads.reshape(grad_ref.shape).astype(grad_ref.dtype)


def share_kernel(part_ref, send_ref, *, devices):
    parts = part_ref[...].astype(F32)
    total = jnp.sum(parts.reshape((devices, -1) + parts.shape[1:]), axis=0, keepdims=True)
    total = jnp.broadcast_to(total.astype(send_ref.dtype), (devices,) + total.shape[1:])
    send_ref[...] = total.reshape(send_ref.shape)


def update_kernel(grad_ref, own_loss_ref, proj_ref, *refs, patches):
    stem_ref, mix_ref, out_ref, proj_update_ref, loss_ref = refs
    loss_ref[...] = own_loss_ref[...]
    value = grad_ref[...].astype(F32).reshape(-1, grad_ref.shape[-1])
    voxels, channels = stem_ref.shape
    embed_dim = proj_ref.shape[0]
    g_stem, g_mix = value[:voxels], value[voxels : voxels + channels]
    factor = value[voxels + channels : voxels + channels + embed_dim].astype(BF16)
    g_out = tn(factor, proj_ref[...]) / patches
    g_proj = value[voxels + channels + embed_dim :]
    for ref, grad in zip((stem_ref, mix_ref, out_ref, proj_update_ref), (g_stem, g_mix, g_out, g_proj)):
        rows = ref.shape[0]
        squares = jnp.sum(jnp.sum(grad * grad, axis=0, keepdims=True), axis=1, keepdims=True)
        ref[...] = grad * lax.rsqrt(squares / (rows * ref.shape[1]) + RMS_EPS)


def vmem(number):
    return [pl.BlockSpec(memory_space=pltpu.VMEM)] * number


def hbm(number):
    return [pl.BlockSpec(memory_space=pltpu.HBM)] * number


def on_device(cutouts, counts, partner, w_stem, w_mix, w_out, w_proj):
    axes = ("rep", "vol")
    owners = lax.axis_size("vol")
    devices = owners * lax.axis_size("rep")
    cut = cutouts[0]
    nodes = cut.shape[0]
    voxels, channels = w_stem.shape
    embed_dim = w_proj.shape[1]
    rows = cut.shape[1] // (2 * voxels) * nodes
    w_proj = w_proj.T
    weights = (w_stem, w_mix, w_out, w_proj)
    shape = jax.ShapeDtypeStruct
    params = pltpu.CompilerParams(vmem_limit_bytes=(16 << 20) + owners * nodes * 8192)

    first = pl.pallas_call(
        first_kernel,
        out_shape=shape((8, 128), F32),
        out_specs=vmem(1)[0],
        compiler_params=params,
        cost_estimate=pl.CostEstimate(flops=10**9, transcendentals=10**6, bytes_accessed=10**8),
        name="first",
    )()
    send, *saved = pl.pallas_call(
        forward_kernel,
        out_shape=(
            shape((owners, nodes // 2, 2 * embed_dim), BF16),
            shape((nodes, channels), BF16),
            shape((nodes, channels), F32),
            shape((nodes, embed_dim), F32),
            shape((nodes, 1), F32),
            shape((2 * channels, rows), BF16),
            shape((2 * voxels, rows), BF16),
            shape((rows, 2 * channels), F32),
            shape((rows, 2 * channels), F32),
            shape(partner.shape, F32),
            shape((2 * channels, 2 * channels), BF16),
            shape(w_out.shape, BF16),
            shape(w_proj.shape, BF16),
        ),
        in_specs=vmem(1) + [pl.BlockSpec(memory_space=pltpu.SMEM)] + vmem(5) + hbm(1),
        out_specs=tuple(vmem(13)),
        scratch_shapes=[pltpu.VMEM(partner.shape, jnp.int32), pltpu.SemaphoreType.DMA(())],
        compiler_params=params,
        name="forward",
    )(first, counts, cut, *weights, pltpu.with_memory_space_constraint(partner, pltpu.HBM))
    pooled, mixed_sum, unit, inv, hidden_t, patch_t, stem_slope, mix_slope, mates, *rest = saved

    gathered = lax.all_to_all(send, "vol", 0, 0).reshape(owners * nodes // 2, 2 * embed_dim)

    total_rows = voxels + channels + 2 * embed_dim
    share = (total_rows + devices - 1) // devices
    tile = next(t for t in (8, 4, 2, 1) if share % t == 0)
    padded = share * devices - total_rows
    parts, loss = pl.pallas_call(
        backward_kernel,
        out_shape=(
            shape((total_rows, channels) if padded else (total_rows // tile, tile, channels), BF16),
            shape((1, partner.shape[1] // owners), F32),
        ),
        in_specs=vmem(13),
        out_specs=tuple(vmem(2)),
        scratch_shapes=[pltpu.VMEM((owners * nodes, embed_dim), BF16)],
        compiler_params=params,
        name="backward",
    )(
        gathered, mates, pooled, mixed_sum, unit, inv,
        hidden_t, patch_t, stem_slope, mix_slope, *rest,
    )
    if padded:
        parts = jnp.pad(parts, ((0, padded), (0, 0))).reshape(-1, tile, channels)
    parts = lax.all_to_all(parts, axes, 0, 0, tiled=True)
    whole = pl.pallas_call(
        lambda *refs: share_kernel(*refs, devices=devices),
        out_shape=shape(parts.shape, BF16),
        in_specs=vmem(1),
        out_specs=vmem(1)[0],
        compiler_params=params,
        name="share",
    )(parts)
    whole = lax.all_to_all(whole, axes, 0, 0, tiled=True)
    if padded:
        whole = whole.reshape(-1, channels)[:total_rows]

    updates = pl.pallas_call(
        lambda *refs: update_kernel(*refs, patches=cut.shape[1] // voxels),
        out_shape=tuple(shape(w.shape, F32) for w in weights) + (shape(loss.shape, F32),),
        in_specs=vmem(3),
        out_specs=tuple(vmem(5)),
        compiler_params=params,
        name="updates",
    )(whole, loss, rest[-1])
    return (*updates[:3], updates[3].T, updates[4][None])


def solution(mesh):
    in_specs = (P("rep", "vol", None), P("rep", "vol"), P("rep", None), P(), P(), P(), P())
    out_specs = (P(), P(), P(), P(), P("rep", "vol", None))
    return jax.shard_map(
        on_device, mesh=mesh, in_specs=in_specs, out_specs=out_specs, check_vma=False
    )
```

```python
import jax
import jax.numpy as jnp
from jax import lax
from jax.experimental import pallas as pl
from jax.experimental.pallas import tpu as pltpu
from jax.sharding import PartitionSpec as P

TEMPERATURE = 0.2
EXPONENT = 1.4426950408889634 / TEMPERATURE
NORM_EPS = 1e-06
RMS_EPS = 1e-06
BF16 = jnp.bfloat16
F32 = jnp.float32
UNUSED = 2.0
GROUP = 16


def nn(left, right):
    return lax.dot_general(left, right, (((1,), (0,)), ((), ())), preferred_element_type=F32)


def nt(left, right):
    return lax.dot_general(left, right, (((1,), (1,)), ((), ())), preferred_element_type=F32)


def tn(left, right):
    return lax.dot_general(left, right, (((0,), (0,)), ((), ())), preferred_element_type=F32)


def split(value):
    high = value.astype(BF16)
    low = (value - high.astype(F32)).astype(BF16)
    return high, low


def paired(weight):
    zero = jnp.zeros_like(weight)
    return jnp.concatenate(
        [
            jnp.concatenate([weight, zero], axis=1),
            jnp.concatenate([zero, weight], axis=1),
        ],
        axis=0,
    )


def pair_rows(cut_ref, width, first, number):
    return jnp.concatenate(
        [cut_ref[:, (first + i) * width : (first + i + 1) * width] for i in range(number)], axis=0
    )


def first_kernel(first_ref):
    first_ref[...] = jnp.zeros(first_ref.shape, first_ref.dtype)


def forward_kernel(
    first_ref, count_ref, cut_ref, stem_ref, mix_ref, out_in, proj_in, partner_hbm,
    send_ref, pooled_ref, mixed_ref, unit_ref, inv_ref, hidden_t_ref, patch_t_ref,
    stem_slope_ref, mix_slope_ref, mate_ref, half_mix_ref, out_ref, proj_ref,
    partner_ref, sem,
):
    nodes = cut_ref.shape[0]
    voxels, channels = stem_ref.shape
    width = 2 * voxels
    blocks = cut_ref.shape[1] // width
    del first_ref
    out_ref[...] = out_in[...]
    proj_ref[...] = proj_in[...]
    partner_copy = pltpu.make_async_copy(partner_hbm, partner_ref, sem)

    def begin(step, carry):
        @pl.when(step == 0)
        def _():
            partner_copy.start()

        return carry

    lax.fori_loop(0, 2, begin, 0)
    stem2 = paired((stem_ref[...].astype(F32) * 0.5).astype(BF16))
    mix2 = paired((mix_ref[...].astype(F32) * 0.5).astype(BF16))
    half_mix_ref[...] = mix2
    hidden_sum = jnp.zeros((nodes, 2 * channels), F32)
    mixed_sum = jnp.zeros((nodes, 2 * channels), F32)
    for first in range(0, blocks, GROUP):
        number = min(GROUP, blocks - first)
        rows = slice(first * nodes, (first + number) * nodes)
        patches = pair_rows(cut_ref, width, first, number)
        half = nn(patches, stem2)
        t = jnp.tanh(half)
        u = 1.0 + t
        hidden = half * u
        stem_slope_ref[rows, :] = u + hidden * (1.0 - t)
        narrow = hidden.astype(BF16)
        half = nn(narrow, mix2)
        t = jnp.tanh(half)
        u = 1.0 + t
        mixed = half * u
        mix_slope_ref[rows, :] = u + mixed * (1.0 - t)
        for i in range(number):
            part = slice(i * nodes, (i + 1) * nodes)
            hidden_sum = hidden_sum + hidden[part]
            mixed_sum = mixed_sum + mixed[part]
        hidden_t_ref[:, rows] = narrow.T
        patch_t_ref[:, rows] = patches.T
    hidden_sum = hidden_sum[:, :channels] + hidden_sum[:, channels:]
    mixed_sum = mixed_sum[:, :channels] + mixed_sum[:, channels:]
    high, low = split(mixed_sum)
    weight = out_ref[...]
    summed = hidden_sum + (nn(high, weight) + nn(low, weight))
    pooled = (summed / (2 * blocks)).astype(BF16)
    raw = nt(pooled, proj_ref[...])
    inv = lax.rsqrt(jnp.sum(raw * raw, axis=1, keepdims=True) + NORM_EPS)
    unit = raw * inv
    count = count_ref[0, 0]
    live = lax.broadcasted_iota(jnp.int32, (nodes, 1), 0) < count
    embed = jnp.where(live, unit, UNUSED)
    send = jnp.concatenate([embed[: nodes // 2], embed[nodes // 2 :]], axis=1).astype(BF16)
    send_ref[...] = jnp.broadcast_to(send[None], send_ref.shape)
    pooled_ref[...] = pooled
    mixed_ref[...] = mixed_sum
    unit_ref[...] = unit
    inv_ref[...] = jnp.where(live, inv, 0.0)

    partner_copy.wait()
    mate_ref[...] = partner_ref[...].astype(F32)


def unpack(gathered_ref, whole_ref, max_nodes):
    slots, embed_dim = whole_ref.shape
    half = max_nodes // 2
    owners = slots // max_nodes
    whole_ref[: slots // 2, :] = gathered_ref[:, :embed_dim]
    whole_ref[slots // 2 :, :] = gathered_ref[:, embed_dim:]
    counts = []
    for owner in range(owners):
        used = gathered_ref[owner * half : (owner + 1) * half, :].astype(F32) < 0.75 * UNUSED
        counts.append(jnp.sum(jnp.where(used, 1.0, 0.0), axis=0, keepdims=True))
    counts = jnp.concatenate(counts, axis=0)
    counts = counts[:, 0:1] + counts[:, embed_dim : embed_dim + 1]
    owner = lax.broadcasted_iota(jnp.int32, (owners, slots), 0)
    slot = lax.broadcasted_iota(jnp.int32, (owners, slots), 1)
    slot_owner = slot % (slots // 2) // half
    count = jnp.sum(jnp.where(owner == slot_owner, counts, 0.0), axis=0, keepdims=True)
    offset = jnp.sum(jnp.where(owner < slot_owner, counts, 0.0), axis=0, keepdims=True)
    slot = lax.broadcasted_iota(jnp.int32, (1, slots), 1)
    within = (slot // (slots // 2) * half + slot % half).astype(F32)
    return within, offset, within < count, counts


def score_sums(whole_ref, live_row):
    slots = whole_ref.shape[0]
    step = min(slots, 256)
    whole = whole_ref[...]

    def block(first, total):
        part = whole_ref[pl.ds(first, step), :]
        scores = nt(part, whole) * EXPONENT
        row = lax.broadcasted_iota(jnp.int32, (step, 1), 0) + first
        live = part[:, 0:1].astype(F32) < 0.75 * UNUSED
        column = lax.broadcasted_iota(jnp.int32, scores.shape, 1)
        keep = jnp.logical_and(live, column != row)
        return total + jnp.sum(jnp.where(keep, jnp.exp2(scores), 0.0), axis=0, keepdims=True)

    total = jnp.zeros((1, slots), F32)
    if slots == step:
        total = block(0, total)
    else:
        total = lax.fori_loop(
            0, slots // step, lambda i, t: block(pl.multiple_of(i * step, step), t), total
        )
    return jnp.where(live_row, total, 1.0)


def look_up(table_ref, number):
    shape = (number.shape[0], table_ref.shape[1])
    listed = lax.broadcasted_iota(jnp.int32, shape, 1).astype(F32)
    return jnp.sum(jnp.where(listed == number, table_ref[...], 0.0), axis=1, keepdims=True)


def backward_kernel(
    gathered_ref, mate_ref, pooled_ref, mixed_ref, unit_ref, inv_ref,
    hidden_t_ref, patch_t_ref, stem_slope_ref, mix_slope_ref, half_mix_ref, out_ref, proj_ref,
    grad_ref, loss_ref, whole_ref,
):
    nodes, embed_dim = unit_ref.shape
    slots = whole_ref.shape[0]
    place = lax.axis_index("vol")
    channels = out_ref.shape[0]
    voxels = patch_t_ref.shape[0] // 2
    blocks = stem_slope_ref.shape[0] // nodes
    half = nodes // 2

    within, offset_row, live_row, counts = unpack(gathered_ref, whole_ref, nodes)
    number_row = jnp.where(live_row, offset_row + within, -1.0)
    totals = score_sums(whole_ref, live_row)

    owner = lax.broadcasted_iota(jnp.int32, counts.shape, 0)
    own_offset = jnp.sum(jnp.where(owner < place, counts, 0.0), axis=0, keepdims=True)
    rank = lax.broadcasted_iota(jnp.int32, (nodes, 1), 0)
    own_number = own_offset + rank.astype(F32)
    mate = look_up(mate_ref, own_number)
    companion = jnp.where(number_row == mate, 1.0, 0.0).astype(BF16)

    whole = whole_ref[...]
    unit = unit_ref[...]
    scores = nt(unit.astype(BF16), whole) * EXPONENT
    own_slot = rank // half * (slots // 2) + place * half + rank % half
    slot_row = lax.broadcasted_iota(jnp.int32, (1, slots), 1)
    other = jnp.logical_and(live_row, slot_row != own_slot)
    weight = jnp.where(other, jnp.exp2(scores), 0.0)
    own_total = jnp.sum(weight, axis=1, keepdims=True)
    row_weight = (weight * (1.0 / own_total)).astype(BF16)
    column_weight = (weight * (1.0 / totals)).astype(BF16)
    mixed_rows = nn(jnp.concatenate([row_weight, column_weight, companion], axis=0), whole)
    d_embed = (
        mixed_rows[:nodes] + mixed_rows[nodes : 2 * nodes] - 2.0 * mixed_rows[2 * nodes :]
    ) / TEMPERATURE

    node_dev = loss_ref.shape[1]
    owners = slots // nodes
    wanted = (lax.broadcasted_iota(jnp.int32, (node_dev, 1), 0) * owners + place).astype(F32)
    mine = number_row == wanted
    total = jnp.sum(jnp.where(mine, totals, 0.0), axis=1, keepdims=True)
    anchor = nn(jnp.where(mine, 1.0, 0.0).astype(BF16), whole)
    other_end = number_row == look_up(mate_ref, wanted)
    other_end = nn(jnp.where(other_end, 1.0, 0.0).astype(BF16), whole)
    loss = jnp.log(total) - jnp.sum(anchor * other_end, axis=1, keepdims=True) / TEMPERATURE
    row = lax.broadcasted_iota(jnp.int32, (node_dev, node_dev), 0)
    column = lax.broadcasted_iota(jnp.int32, (node_dev, node_dev), 1)
    loss_ref[...] = jnp.sum(jnp.where(row == column, loss, 0.0), axis=0, keepdims=True)

    radial = jnp.sum(unit * d_embed, axis=1, keepdims=True)
    d_raw = (inv_ref[...] * (d_embed - unit * radial)).astype(BF16)
    g_proj = tn(d_raw, pooled_ref[...])
    d_sum = (nn(d_raw, proj_ref[...]) / (2 * blocks)).astype(BF16)
    high, low = split(mixed_ref[...])
    g_out = tn(high, d_sum) + tn(low, d_sum)
    d_mixed = 0.5 * nt(d_sum, out_ref[...])
    d_mixed = jnp.concatenate([d_mixed, d_mixed], axis=1)
    d_pool = 0.5 * d_sum.astype(F32)
    d_pool = jnp.concatenate([d_pool, d_pool], axis=1)
    half_mix = half_mix_ref[...]

    g_mix = jnp.zeros((2 * channels, 2 * channels), F32)
    g_stem = jnp.zeros((2 * voxels, 2 * channels), F32)
    chunk = 2 * GROUP
    for first in range(0, blocks, chunk):
        number = min(chunk, blocks - first)
        rows = slice(first * nodes, (first + number) * nodes)
        d_pre_mix = jnp.concatenate(
            [
                (d_mixed * mix_slope_ref[(first + i) * nodes : (first + i + 1) * nodes, :]).astype(BF16)
                for i in range(number)
            ],
            axis=0,
        )
        g_mix = g_mix + nn(hidden_t_ref[:, rows], d_pre_mix)
        back = nt(d_pre_mix, half_mix)
        d_pre_stem = jnp.concatenate(
            [
                (
                    (d_pool + back[i * nodes : (i + 1) * nodes])
                    * stem_slope_ref[(first + i) * nodes : (first + i + 1) * nodes, :]
                ).astype(BF16)
                for i in range(number)
            ],
            axis=0,
        )
        g_stem = g_stem + nn(patch_t_ref[:, rows], d_pre_stem)
    g_mix = g_mix[:channels, :channels] + g_mix[channels:, channels:]
    g_stem = g_stem[:voxels, :channels] + g_stem[voxels:, channels:]
    grads = jnp.concatenate([g_stem, g_mix, g_out, g_proj], axis=0)
    grad_ref[...] = grads.reshape(grad_ref.shape).astype(grad_ref.dtype)


def share_kernel(part_ref, send_ref, *, devices):
    parts = part_ref[...].astype(F32)
    total = jnp.sum(parts.reshape((devices, -1) + parts.shape[1:]), axis=0, keepdims=True)
    total = jnp.broadcast_to(total.astype(send_ref.dtype), (devices,) + total.shape[1:])
    send_ref[...] = total.reshape(send_ref.shape)


def update_kernel(grad_ref, own_loss_ref, *refs):
    *refs, loss_ref = refs
    loss_ref[...] = own_loss_ref[...]
    value = grad_ref[...].astype(F32).reshape(-1, grad_ref.shape[-1])
    start = 0
    for ref in refs:
        rows = ref.shape[0]
        grad = value[start : start + rows]
        start += rows
        squares = jnp.sum(jnp.sum(grad * grad, axis=0, keepdims=True), axis=1, keepdims=True)
        ref[...] = grad * lax.rsqrt(squares / (rows * ref.shape[1]) + RMS_EPS)


def vmem(number):
    return [pl.BlockSpec(memory_space=pltpu.VMEM)] * number


def hbm(number):
    return [pl.BlockSpec(memory_space=pltpu.HBM)] * number


def on_device(cutouts, counts, partner, w_stem, w_mix, w_out, w_proj):
    axes = ("rep", "vol")
    owners = lax.axis_size("vol")
    devices = owners * lax.axis_size("rep")
    cut = cutouts[0]
    nodes = cut.shape[0]
    voxels, channels = w_stem.shape
    embed_dim = w_proj.shape[1]
    rows = cut.shape[1] // (2 * voxels) * nodes
    w_proj = w_proj.T
    weights = (w_stem, w_mix, w_out, w_proj)
    shape = jax.ShapeDtypeStruct
    params = pltpu.CompilerParams(vmem_limit_bytes=(16 << 20) + owners * nodes * 8192)

    first = pl.pallas_call(
        first_kernel,
        out_shape=shape((8, 128), F32),
        out_specs=vmem(1)[0],
        compiler_params=params,
        cost_estimate=pl.CostEstimate(flops=10**9, transcendentals=10**6, bytes_accessed=10**8),
        name="first",
    )()
    send, *saved = pl.pallas_call(
        forward_kernel,
        out_shape=(
            shape((owners, nodes // 2, 2 * embed_dim), BF16),
            shape((nodes, channels), BF16),
            shape((nodes, channels), F32),
            shape((nodes, embed_dim), F32),
            shape((nodes, 1), F32),
            shape((2 * channels, rows), BF16),
            shape((2 * voxels, rows), BF16),
            shape((rows, 2 * channels), F32),
            shape((rows, 2 * channels), F32),
            shape(partner.shape, F32),
            shape((2 * channels, 2 * channels), BF16),
            shape(w_out.shape, BF16),
            shape(w_proj.shape, BF16),
        ),
        in_specs=vmem(1) + [pl.BlockSpec(memory_space=pltpu.SMEM)] + vmem(5) + hbm(1),
        out_specs=tuple(vmem(13)),
        scratch_shapes=[pltpu.VMEM(partner.shape, jnp.int32), pltpu.SemaphoreType.DMA(())],
        compiler_params=params,
        name="forward",
    )(first, counts, cut, *weights, pltpu.with_memory_space_constraint(partner, pltpu.HBM))
    pooled, mixed_sum, unit, inv, hidden_t, patch_t, stem_slope, mix_slope, mates, *rest = saved

    gathered = lax.all_to_all(send, "vol", 0, 0).reshape(owners * nodes // 2, 2 * embed_dim)

    total_rows = sum(w.shape[0] for w in weights)
    share = (total_rows + devices - 1) // devices
    tile = next(t for t in (8, 4, 2, 1) if share % t == 0)
    padded = share * devices - total_rows
    parts, loss = pl.pallas_call(
        backward_kernel,
        out_shape=(
            shape((total_rows, channels) if padded else (total_rows // tile, tile, channels), BF16),
            shape((1, partner.shape[1] // owners), F32),
        ),
        in_specs=vmem(13),
        out_specs=tuple(vmem(2)),
        scratch_shapes=[pltpu.VMEM((owners * nodes, embed_dim), BF16)],
        compiler_params=params,
        name="backward",
    )(
        gathered, mates, pooled, mixed_sum, unit, inv,
        hidden_t, patch_t, stem_slope, mix_slope, *rest,
    )
    if padded:
        parts = jnp.pad(parts, ((0, padded), (0, 0))).reshape(-1, tile, channels)
    parts = lax.all_to_all(parts, axes, 0, 0, tiled=True)
    whole = pl.pallas_call(
        lambda *refs: share_kernel(*refs, devices=devices),
        out_shape=shape(parts.shape, BF16),
        in_specs=vmem(1),
        out_specs=vmem(1)[0],
        compiler_params=params,
        name="share",
    )(parts)
    whole = lax.all_to_all(whole, axes, 0, 0, tiled=True)
    if padded:
        whole = whole.reshape(-1, channels)[:total_rows]

    updates = pl.pallas_call(
        update_kernel,
        out_shape=tuple(shape(w.shape, F32) for w in weights) + (shape(loss.shape, F32),),
        in_specs=vmem(2),
        out_specs=tuple(vmem(5)),
        compiler_params=params,
        name="updates",
    )(whole, loss)
    return (*updates[:3], updates[3].T, updates[4][None])


def solution(mesh):
    in_specs = (P("rep", "vol", None), P("rep", "vol"), P("rep", None), P(), P(), P(), P())
    out_specs = (P(), P(), P(), P(), P("rep", "vol", None))
    return jax.shard_map(
        on_device, mesh=mesh, in_specs=in_specs, out_specs=out_specs, check_vma=False
    )
```
